32 devices in a mesh: seq: 2 (over core), head: 2 (over y), blk: 8 (over z, x).
Axes of the slice: x: 2, y: 2, z: 4, core: 2. Of those that a mesh axis runs over, the one named last changes fastest.
Arguments:
- stream: bfloat16 [4096, 2048], P(('seq', 'head', 'blk')), may hold values from -6 to 6
- attn_gain: bfloat16 [2048], P(('seq', 'head', 'blk')), may hold values from 0.5 to 1.5
- qkv_weight: bfloat16 [2048, 2560], P(('seq', 'head', 'blk')), may hold values from -0.125 to 0.125
- qkv_adapt: bfloat16 [2048, 256], P(('seq', 'head', 'blk')), may hold values from -0.125 to 0.125
- qkv_expand: bfloat16 [256, 2560], P(('seq', 'head', 'blk')), may hold values from -0.375 to 0.375
- out_weight: bfloat16 [2048, 2048], P(('seq', 'head', 'blk')), may hold values from -1 to 1
- out_adapt: bfloat16 [2048, 256], P(('seq', 'head', 'blk')), may hold values from -1 to 1
- out_expand: bfloat16 [256, 2048], P(('seq', 'head', 'blk')), may hold values from -0.375 to 0.375
- ffn_gain: bfloat16 [2048], P(('seq', 'head', 'blk')), may hold values from 0.5 to 1.5
- gateup_weight: bfloat16 [16384, 2, 2048], P(('seq', 'head', 'blk')), may hold values from -0.125 to 0.125
- gateup_adapt: bfloat16 [2048, 256], P(('seq', 'head', 'blk')), may hold values from -0.125 to 0.125
- gateup_expand: bfloat16 [16384, 2, 256], P(('seq', 'head', 'blk')), may hold values from -0.375 to 0.375
- down_weight: bfloat16 [16384, 2048], P(('seq', 'head', 'blk')), may hold values from -0.046875 to 0.046875
- down_adapt: bfloat16 [16384, 256], P(('seq', 'head', 'blk')), may hold values from -0.046875 to 0.046875
- down_expand: bfloat16 [256, 2048], P(('seq', 'head', 'blk')), may hold values from -0.375 to 0.375
- cotangent: bfloat16 [4096, 2048], P(('seq', 'head', 'blk')), may hold values from -6 to 6
Outputs:
- result: bfloat16 [4096, 2048], P(('seq', 'head', 'blk'))
- stream_grad: float32 [4096, 2048], P(('seq', 'head', 'blk'))
- attngain_grad: float32 [2048], P(('seq', 'head', 'blk'))
- qkvweight_grad: float32 [2048, 2560], P(('seq', 'head', 'blk'))
- qkvadapt_grad: float32 [2048, 256], P(('seq', 'head', 'blk'))
- qkvexpand_grad: float32 [256, 2560], P(('seq', 'head', 'blk'))
- outweight_grad: float32 [2048, 2048], P(('seq', 'head', 'blk'))
- outadapt_grad: float32 [2048, 256], P(('seq', 'head', 'blk'))
- outexpand_grad: float32 [256, 2048], P(('seq', 'head', 'blk'))
- ffngain_grad: float32 [2048], P(('seq', 'head', 'blk'))
- gateweight_grad: float32 [16384, 2, 2048], P(('seq', 'head', 'blk'))
- gateadapt_grad: float32 [2048, 256], P(('seq', 'head', 'blk'))
- gateexpand_grad: float32 [16384, 2, 256], P(('seq', 'head', 'blk'))
- downweight_grad: float32 [16384, 2048], P(('seq', 'head', 'blk'))
- downadapt_grad: float32 [16384, 256], P(('seq', 'head', 'blk'))
- downexpand_grad: float32 [256, 2048], P(('seq', 'head', 'blk'))
- root_means: float32 [3, 4096], P(None, ('seq', 'head', 'blk'))
The draws below stay inside these ranges and needn't reach their ends.
All inputs are finite; a program needn't handle non-finite values.
Results may differ from the reference program's by a relative error of at most 0.023.
Values may be sent and summed in bfloat16 or wider, within the bound.
No kernel may reach another device: no remote copies, remote signals or barrier semaphores. Data moves between devices by JAX's collectives and lax.ppermute only.
A program may use at most 320 MiB of HBM per device.

```python
import math
import jax
import jax.numpy as jnp
from jax import lax

D = 2048
H = 8
DH = 256
FF = 16384
R = 256
HD = 2048
QKV = 2560
SEQ = 2048
TOKENS = 4096
N_SEQ = 2


def levels(stream_key, dims, split, least, largest):
    factor_of = 1.0
    for position, blocks in split:
        steps = jax.random.uniform(jax.random.fold_in(jax.random.fold_in(stream_key, 6), position), (blocks,), jnp.float32, least / len(split), largest / len(split))
        factor_of = factor_of * jnp.repeat(jnp.exp(steps), dims[position] // blocks).reshape((-1,) + (1,) * (len(dims) - 1 - position))
    return factor_of


def centred(own_key, dims, spread, reach, cuts=(), held_as=jnp.bfloat16):
    result = spread * jax.random.normal(own_key, dims, jnp.float32)
    if cuts:
        result = result * levels(own_key, dims, cuts, -0.22, 0.18)
    return jnp.clip(result, -reach, reach).astype(held_as)


def setup_inputs(seed: int = 0) -> dict:
    arg_keys = jax.random.split(jax.random.key(seed), 17)
    stream = centred(arg_keys[0], (TOKENS, D), 1.0, 6.0, ((0, 32),))
    attn_gain = jnp.clip(1.0 + 0.1 * jax.random.normal(arg_keys[1], (D,), jnp.float32), 0.5, 1.5).astype(jnp.bfloat16)
    qkv_weight = centred(arg_keys[2], (D, QKV), D ** -0.5, 0.125, ((0, 32),))
    qkv_adapt = centred(arg_keys[3], (D, R), D ** -0.5, 0.125, ((0, 32),))
    qkv_expand = centred(arg_keys[4], (R, QKV), R ** -0.5, 0.375, ((0, 32),))
    out_weight = centred(arg_keys[5], (HD, D), (HD // 64) ** -0.5, 1.0, ((0, 32),))
    out_adapt = centred(arg_keys[6], (HD, R), (HD // 64) ** -0.5, 1.0, ((0, 32),))
    out_expand = centred(arg_keys[7], (R, D), R ** -0.5, 0.375, ((0, 32),))
    ffn_gain = jnp.clip(1.0 + 0.1 * jax.random.normal(arg_keys[8], (D,), jnp.float32), 0.5, 1.5).astype(jnp.bfloat16)
    gateup_weight = centred(arg_keys[9], (FF, 2, D), D ** -0.5, 0.125, ((0, 32),))
    gateup_adapt = centred(arg_keys[10], (D, R), D ** -0.5, 0.125, ((0, 32),))
    gateup_expand = centred(arg_keys[11], (FF, 2, R), R ** -0.5, 0.375, ((0, 32),))
    down_weight = centred(arg_keys[12], (FF, D), FF ** -0.5, 0.046875, ((0, 32),))
    down_adapt = centred(arg_keys[13], (FF, R), FF ** -0.5, 0.046875, ((0, 32),))
    down_expand = centred(arg_keys[14], (R, D), R ** -0.5, 0.375, ((0, 32),))
    cotangent = centred(arg_keys[15], (TOKENS, D), 1.0, 6.0, ((0, 32),))
    return {"stream": stream, "attn_gain": attn_gain, "qkv_weight": qkv_weight, "qkv_adapt": qkv_adapt, "qkv_expand": qkv_expand, "out_weight": out_weight, "out_adapt": out_adapt, "out_expand": out_expand, "ffn_gain": ffn_gain, "gateup_weight": gateup_weight, "gateup_adapt": gateup_adapt, "gateup_expand": gateup_expand, "down_weight": down_weight, "down_adapt": down_adapt, "down_expand": down_expand, "cotangent": cotangent}


EPSILON = 1e-06
NEGATIVE = -1e+30
HIGH = lax.Precision.HIGHEST

@jax.custom_vjp
def low(v):
    return lax.optimization_barrier(v.astype(jnp.bfloat16)).astype(jnp.float32)

@jax.custom_vjp
def low_back(v):
    return v

def low_keep(v):
    return (low(v), None)

def low_pass(kept, grad):
    return (grad,)

def back_keep(v):
    return (v, None)

def back_low(kept, grad):
    return (low(grad),)
low.defvjp(low_keep, low_pass)
low_back.defvjp(back_keep, back_low)

def product(former, latter):
    return jnp.dot(former, latter, precision=HIGH, preferred_element_type=jnp.float32)

def normalize(values, gain_row):
    return values * lax.rsqrt(lax.optimization_barrier(jnp.mean(values * values, axis=-1, keepdims=True)) + EPSILON) * gain_row

def rope_tables(positions, full_width):
    half_width = full_width // 2
    rates = jnp.exp(jnp.arange(half_width, dtype=jnp.float32) * (-2.0 * math.log(10000.0) / full_width))
    angles = positions.astype(jnp.float32)[:, None] * rates[None, :]
    return (jnp.cos(angles), jnp.sin(angles))

def rotate(values, cosine, sine_part):
    half_width = values.shape[-1] // 2
    former = values[..., :half_width]
    latter = values[..., half_width:]
    return jnp.concatenate([former * cosine - latter * sine_part, latter * cosine + former * sine_part], axis=-1)

def root_mean(values):
    return jnp.sqrt(lax.optimization_barrier(jnp.mean(values * values, axis=-1)))

def block_layer(stream, params, positions):
    attn_gain, qkv_weight, qkv_adapt, qkv_expand, out_weight, out_adapt, out_expand, ffn_gain, gateup_weight, gateup_adapt, gateup_expand, down_weight, down_adapt, down_expand = params
    length = stream.shape[0]
    normed_one = low(normalize(stream, attn_gain))
    lowrank_one = low(low_back(product(normed_one, qkv_adapt)))
    joined = low_back(product(normed_one, qkv_weight) + product(lowrank_one, qkv_expand))
    cosine, sine_part = rope_tables(positions, DH)
    queries = low(rotate(joined[:, :H * DH].reshape(length, H, DH), cosine[:, None, :], sine_part[:, None, :]))
    keys = low(rotate(joined[:, H * DH:H * DH + DH], cosine, sine_part))
    values = low(joined[:, H * DH + DH:])
    row_block = min(512, length)
    score_scale = DH ** (-0.5)
    key_pos = jnp.arange(length, dtype=jnp.int32)

    def attend(first_row):
        query_rows = lax.dynamic_slice_in_dim(queries, first_row, row_block, 0)
        scores = low_back(jnp.einsum('bhe,le->bhl', query_rows, keys, precision=HIGH) * score_scale)
        query_pos = first_row + jnp.arange(row_block, dtype=jnp.int32)
        visible = key_pos[None, None, :] <= query_pos[:, None, None]
        scores = jnp.where(visible, scores, NEGATIVE)
        row_top = lax.optimization_barrier(jnp.max(scores, axis=-1, keepdims=True))
        raised = jnp.where(visible, jnp.exp(scores - row_top), 0.0)
        shares = raised / lax.optimization_barrier(jnp.sum(raised, axis=-1, keepdims=True))
        return jnp.einsum('bhl,le->bhe', low(shares), values, precision=HIGH)
    starts = jnp.arange(length // row_block, dtype=jnp.int32) * row_block
    attended = lax.map(jax.checkpoint(attend), starts).reshape(length, H * DH)
    attn_rows = low(low_back(attended))
    lowrank_two = low(low_back(product(attn_rows, out_adapt)))
    branch_attn = low_back(product(attn_rows, out_weight) + product(lowrank_two, out_expand))
    middle = stream + branch_attn
    normed_two = low(normalize(middle, ffn_gain))
    lowrank_three = low(low_back(product(normed_two, gateup_adapt)))
    gate_up = low_back(jnp.einsum('td,nkd->tkn', normed_two, gateup_weight, precision=HIGH) + jnp.einsum('tr,nkr->tkn', lowrank_three, gateup_expand, precision=HIGH))
    hidden = low(jax.nn.gelu(gate_up[:, 0], approximate=True) * gate_up[:, 1])
    lowrank_four = low(low_back(product(hidden, down_adapt)))
    branch_ffn = low_back(product(hidden, down_weight) + product(lowrank_four, down_expand))
    return (middle + branch_ffn, (branch_attn, branch_ffn))

def reference(stream, attn_gain, qkv_weight, qkv_adapt, qkv_expand, out_weight, out_adapt, out_expand, ffn_gain, gateup_weight, gateup_adapt, gateup_expand, down_weight, down_adapt, down_expand, cotangent):
    params = tuple((weight.astype(jnp.float32) for weight in (attn_gain, qkv_weight, qkv_adapt, qkv_expand, out_weight, out_adapt, out_expand, ffn_gain, gateup_weight, gateup_adapt, gateup_expand, down_weight, down_adapt, down_expand)))
    length = SEQ
    inputs = stream.astype(jnp.float32).reshape(N_SEQ, length, D)
    cotangents = cotangent.astype(jnp.float32).reshape(N_SEQ, length, D)
    positions = jnp.arange(length, dtype=jnp.int32)

    def one_sequence(totals, pair_rows):
        rows_in, rows_back = pair_rows

        def forward(tokens_in, weights_in):
            return block_layer(tokens_in, weights_in, positions)
        output, pullback, branches = jax.vjp(forward, rows_in, params, has_aux=True)
        grad_rows, grad_params = pullback(rows_back)
        statistics = jnp.stack([root_mean(output), root_mean(branches[0]), root_mean(branches[1])])
        totals = tuple((total_grad + new_grad for total_grad, new_grad in zip(totals, grad_params)))
        return (totals, (output.astype(jnp.bfloat16), grad_rows, statistics))
    start_totals = tuple((jnp.zeros_like(weight) for weight in params))
    totals, (outputs, grad_rows, statistics) = lax.scan(one_sequence, start_totals, (inputs, cotangents))
    return (outputs.reshape(N_SEQ * length, D), grad_rows.reshape(N_SEQ * length, D), totals[0], totals[1], totals[2], totals[3], totals[4], totals[5], totals[6], totals[7], totals[8], totals[9], totals[10], totals[11], totals[12], totals[13], jnp.transpose(statistics, (1, 0, 2)).reshape(3, N_SEQ * length))
```

```python
import functools
import math

import jax
import jax.numpy as jnp
from jax import lax
from jax.sharding import PartitionSpec as P

D = 2048
H = 8
DH = 256
R = 256


EPSILON = 1e-06
NEGATIVE = -1e30


def product(former, latter):
    return jnp.dot(former, latter, preferred_element_type=jnp.float32)


def product_back(former, latter):
    return lax.dot_general(
        former, latter, (((1,), (1,)), ((), ())), preferred_element_type=jnp.float32
    )


def product_rows(former, latter):
    return lax.dot_general(
        former, latter, (((0,), (0,)), ((), ())), preferred_element_type=jnp.float32
    )


def rope_tables(positions, full_width):
    half_width = full_width // 2
    rates = jnp.exp(
        jnp.arange(half_width, dtype=jnp.float32) * (-2.0 * math.log(10000.0) / full_width)
    )
    angles = positions.astype(jnp.float32)[:, None] * rates[None, :]
    return (jnp.cos(angles), jnp.sin(angles))


def rotate(values, cosine, sine_part):
    half_width = values.shape[-1] // 2
    former = values[..., :half_width]
    latter = values[..., half_width:]
    return jnp.concatenate(
        [former * cosine - latter * sine_part, latter * cosine + former * sine_part], axis=-1
    )


def unit_rows(values):
    inverse = lax.rsqrt(jnp.mean(values * values, axis=-1, keepdims=True) + EPSILON)
    return (values * inverse, inverse)


def norm_back(grad_in, scaled_rows, inverse, gain_row):
    weighted = grad_in * gain_row
    return inverse * (
        weighted - scaled_rows * jnp.mean(weighted * scaled_rows, axis=-1, keepdims=True)
    )


def root_mean(values):
    return jnp.sqrt(jnp.mean(values * values, axis=-1))


def shift(values, axes, mask):
    size = lax.axis_size(axes)
    return lax.ppermute(values, axes, [(i, i ^ mask) for i in range(size)])


def place(own, other, axis_name, position):
    first = lax.axis_index(axis_name) == 0
    return jnp.stack(
        [jnp.where(first, own, other), jnp.where(first, other, own)], axis=position
    )


class Gather:
    def __init__(self, shard, order, ranking):
        self.value, self.order, self.ranking = shard, list(order), ranking
        self.tail, self.done = shard.shape[1:], []

    def start(self):
        return shift(self.value, self.order[0], 1)

    def finish(self, other):
        name = self.order.pop(0)
        position = sum(self.ranking.index(d) < self.ranking.index(name) for d in self.done)
        self.value = place(self.value, other, name, position)
        self.done.append(name)

    def result(self):
        return self.value.reshape((-1,) + self.tail)


class Scatter:
    def __init__(self, terms, order, ranking):
        self.left = [name for name in ranking if name in order]
        self.order = list(order)
        rows = terms.shape[0] // 2 ** len(order)
        self.value = terms.reshape((2,) * len(order) + (rows,) + terms.shape[1:])

    def start(self):
        name = self.order[0]
        position, mine = self.left.index(name), lax.axis_index(name)
        sent = lax.dynamic_index_in_dim(self.value, 1 - mine, position, keepdims=False)
        return shift(sent, name, 1)

    def finish(self, other):
        name = self.order.pop(0)
        position, mine = self.left.index(name), lax.axis_index(name)
        kept = lax.dynamic_index_in_dim(self.value, mine, position, keepdims=False)
        self.value = kept.astype(jnp.float32) + other.astype(jnp.float32)
        if self.order:
            self.value = self.value.astype(jnp.bfloat16)
        self.left.remove(name)

    def result(self):
        return self.value


class ScatterNear(Scatter):
    def start(self):
        position = self.left.index(self.order[0])
        sent = lax.index_in_dim(self.value, 1, position, keepdims=False)
        return shift(sent, self.order[0], 1)

    def finish(self, other):
        name = self.order.pop(0)
        kept = lax.index_in_dim(self.value, 0, self.left.index(name), keepdims=False)
        self.value = kept.astype(jnp.float32) + other.astype(jnp.float32)
        if self.order:
            self.value = self.value.astype(jnp.bfloat16)
        self.left.remove(name)


def advance(*jobs, beside=()):
    arrived, beside = lax.optimization_barrier(([job.start() for job in jobs], beside))
    for job, other in zip(jobs, arrived):
        job.finish(other)
    return arrived, beside


def tie(values, *others):
    return lax.optimization_barrier((values, others))[0]


def body(
    ranking,
    stream,
    attn_gain,
    qkv_weight,
    qkv_adapt,
    qkv_expand,
    out_weight,
    out_adapt,
    out_expand,
    ffn_gain,
    gateup_weight,
    gateup_adapt,
    gateup_expand,
    down_weight,
    down_adapt,
    down_expand,
    cotangent,
):
    bf16 = jnp.bfloat16
    f32 = jnp.float32
    tokens = stream.shape[0]
    highs, low = ranking[2:-1], ranking[-1]
    row_axes, block_axes, unit_axes = ranking[1:], ranking[2:], ranking[:2]
    upper, mid, core = highs[:-1], highs[-1:], ("seq",)
    orders = (
        ("head",) + upper + (low,) + mid,
        ("head",) + mid + (low,) + upper,
        upper + ("head",) + mid + (low,),
        mid + ("head",) + upper + (low,),
    )
    steps = len(orders[0])
    backs = tuple(order[::-1] for order in orders)
    group = lax.axis_size(row_axes)
    planes = lax.axis_size(highs)
    plane = lax.axis_index(highs)
    side = lax.axis_index(low)
    own_pos = lax.axis_index(row_axes) * tokens + jnp.arange(tokens, dtype=jnp.int32)
    score_scale = DH ** (-0.5)
    half = H * DH // 2
    rank_rows = qkv_expand.shape[0]
    gain_columns = attn_gain.shape[0] // rank_rows

    from_row = jnp.concatenate(
        [
            qkv_expand,
            out_expand,
            down_expand,
            attn_gain.reshape(rank_rows, gain_columns),
            ffn_gain.reshape(rank_rows, gain_columns),
            jnp.zeros((rank_rows, 128 - 2 * gain_columns), bf16),
        ],
        axis=1,
    )
    jobs = [
        Gather(shard, order + core, ranking)
        for shard, order in zip(
            (
                jnp.concatenate([qkv_weight[:, 2 * half :], qkv_adapt], axis=1),
                from_row,
                qkv_weight[:, :half],
                qkv_weight[:, half : 2 * half],
            ),
            orders,
        )
    ]
    def gather_units(block):
        return lax.all_gather(block, unit_axes, axis=0, tiled=True)

    down_all = gather_units(jnp.concatenate([down_weight, down_adapt], axis=1))
    arrived, _ = advance(*jobs)
    pair_weight, pair_expand = tie((gateup_weight, gateup_expand), arrived)
    pairs = [
        jnp.concatenate([pair_weight[:, k], pair_expand[:, k]], axis=1) for k in range(2)
    ]
    arrived, pairs = advance(*jobs, beside=pairs)
    for _ in range(steps - 3):
        arrived, _ = advance(*jobs)
    gate_all = gather_units(tie(pairs[0], arrived))
    arrived, down_all = advance(*jobs, beside=down_all)
    advance(*jobs)
    kv_into, from_all, query_one, query_two = (job.result() for job in jobs)
    kv_full, qkv_into = kv_into[:, : 2 * DH], kv_into[:, 2 * DH :]
    qkv_columns = 2 * half + 2 * DH
    qkv_from = from_all[:, :qkv_columns]
    proj_from = from_all[:, qkv_columns : qkv_columns + D]
    down_from = from_all[:, qkv_columns + D : qkv_columns + 2 * D]
    gains = from_all[:, qkv_columns + 2 * D :]
    gain_one = gains[:, :gain_columns].reshape(D).astype(f32)
    gain_two = gains[:, gain_columns : 2 * gain_columns].reshape(D).astype(f32)

    residual = stream.astype(f32)
    unit_one, inverse_one = unit_rows(residual)
    normed_one = (unit_one * gain_one).astype(bf16)
    lowrank_one = product(normed_one, qkv_into).astype(bf16)
    joined_kv = product(normed_one, kv_full) + product(lowrank_one, qkv_from[:, 2 * half :])
    cosine, sine_part = rope_tables(own_pos, DH)
    keys = rotate(joined_kv[:, :DH], cosine, sine_part).astype(bf16)
    values = joined_kv[:, DH:].astype(bf16)
    joined_q = jnp.concatenate(
        [product(normed_one, query_one), product(normed_one, query_two)], axis=1
    ) + product(lowrank_one, qkv_from[:, : 2 * half])
    queries = (
        rotate(jnp.stack(jnp.split(joined_q, H, axis=1)), cosine, sine_part)
        .astype(bf16)
        .reshape(H * tokens, DH)
    )

    jobs = [
        Gather(shard, order, ranking)
        for shard, order in zip(
            (
                keys,
                values,
                jnp.concatenate([out_weight[:, :half], out_adapt], axis=1),
                jnp.concatenate([out_weight[:, half:], gateup_adapt], axis=1),
            ),
            (orders[1], orders[3], orders[0] + core, orders[2] + core),
        )
    ]
    arrived, (queries, gate_all) = advance(*jobs, beside=(queries, gate_all))
    up_all = gather_units(tie(pairs[1], gate_all))
    for _ in range(steps - 2):
        arrived, _ = advance(*jobs)
    arrived, up_all = advance(*jobs, beside=up_all)
    keys_all, values_all = jobs[0].result(), jobs[1].result()
    advance(*jobs[2:])
    out_one, out_two = jobs[2].result(), jobs[3].result()
    proj_one, proj_into = out_one[:, :half], out_one[:, half:]
    proj_two, ffn_into = out_two[:, :half], out_two[:, half:]

    def gather_near(rows):
        return [rows] + [shift(rows, highs, mask) for mask in range(1, planes)]

    def to_relative(rows):
        return jnp.concatenate(
            [
                lax.dynamic_slice_in_dim(
                    rows, ((plane ^ mask) * 2 + (side ^ far)) * tokens, tokens, 0
                )
                for far in range(2)
                for mask in range(planes)
            ],
            axis=0,
        )

    def to_absolute(rows):
        return jnp.concatenate(
            [
                lax.dynamic_slice_in_dim(
                    rows, ((side ^ far) * planes + (plane ^ mask)) * tokens, tokens, 0
                )
                for mask in range(planes)
                for far in range(2)
            ],
            axis=0,
        )

    key_pos = jnp.arange(group * tokens, dtype=jnp.int32)
    pieces = max(1, group * tokens // 2048)
    piece_rows = H * tokens // pieces
    visible = jnp.tile(key_pos[None, :] <= own_pos[:, None], (H // pieces, 1))

    def shares_of(query_rows):
        scores = jnp.where(
            visible, product_back(query_rows, keys_all) * score_scale, NEGATIVE
        )
        row_top = jnp.max(scores, axis=-1, keepdims=True)
        raised = jnp.where(visible, jnp.exp(scores - row_top), 0.0)
        return raised / jnp.sum(raised, axis=-1, keepdims=True)

    query_parts = jnp.split(queries, pieces, axis=0)
    kept, attended_parts = [], []
    for query_rows in query_parts:
        shares = shares_of(query_rows)
        attended_parts.append(product(shares.astype(bf16), values_all))
        if pieces == 1:
            kept.append(shares)

    def to_rows(parts):
        return jnp.concatenate(jnp.split(parts, H, axis=0), axis=1)

    def to_heads(rows):
        return jnp.concatenate(jnp.split(rows, H, axis=1), axis=0)

    attn_rows = to_rows(jnp.concatenate(attended_parts, axis=0).astype(bf16))
    lowrank_two = product(attn_rows, proj_into).astype(bf16)
    branch_attn = jnp.concatenate(
        [product(attn_rows, proj_one), product(attn_rows, proj_two)], axis=1
    ) + product(lowrank_two, proj_from)
    middle = residual + branch_attn
    unit_two, inverse_two = unit_rows(middle)
    normed_two = (unit_two * gain_two).astype(bf16)

    near = gather_near(normed_two)
    rows_group = jnp.concatenate(near + [shift(piece, low, 1) for piece in near], axis=0)
    back_all = lax.all_gather(
        tie(cotangent, near[1:], up_all), block_axes, axis=0, tiled=True
    )
    low_group = product(rows_group, ffn_into).astype(bf16)
    rows_joined = jnp.concatenate([rows_group, low_group], axis=1)
    gate = product_back(rows_joined, gate_all)
    up = product_back(rows_joined, up_all)
    hidden = (jax.nn.gelu(gate, approximate=True) * up).astype(bf16)
    out_terms = to_absolute(product(hidden, down_all).astype(bf16))
    mixed = lax.psum_scatter(
        tie(out_terms, back_all), block_axes, scatter_dimension=0, tiled=True
    )
    back_rows = tie(to_relative(back_all), out_terms)
    back_low = product_back(back_rows, down_from).astype(bf16)
    back_joined = jnp.concatenate([back_rows, back_low], axis=1)
    grad_hidden = product_back(back_joined, down_all)
    _, pullback = jax.vjp(lambda a, b: jax.nn.gelu(a, approximate=True) * b, gate, up)
    grad_gate, grad_up = (term.astype(bf16) for term in pullback(grad_hidden))

    row_terms = (product(grad_gate, gate_all) + product(grad_up, up_all)).astype(bf16)
    middle_column = row_terms.shape[1] // 2
    jobs = [
        ScatterNear(row_terms[:, :middle_column], (low,) + mid + upper, (low,) + highs),
        ScatterNear(row_terms[:, middle_column:], mid + upper + (low,), (low,) + highs),
    ]
    def scatter_units(terms):
        return lax.psum_scatter(terms, unit_axes, scatter_dimension=0, tiled=True)

    hidden_late, gate_late = tie((hidden, grad_gate), row_terms)
    work = (
        product_rows(hidden_late, back_joined).astype(bf16),
        product_rows(gate_late, rows_joined).astype(bf16),
    )
    arrived, (down_terms, gate_terms) = advance(*jobs, beside=work)
    up_terms = product_rows(tie(grad_up, arrived), rows_joined).astype(bf16)
    _, (up_terms, mixed) = advance(*jobs, beside=(up_terms, mixed))
    down_sum = scatter_units(tie(down_terms, mixed))
    mixed = mixed.astype(f32)
    for _ in range(len(highs) - 1):
        advance(*jobs)
    parts = jnp.concatenate([job.result() for job in jobs], axis=1)

    lowrank_four = mixed[:, D:].astype(bf16)
    branch_ffn = mixed[:, :D] + product(lowrank_four, down_from)
    final = middle + branch_ffn
    result = final.astype(bf16)
    root_means = jnp.stack([root_mean(final), root_mean(branch_attn), root_mean(branch_ffn)])
    expand_down = product_rows(lowrank_four, cotangent)

    grad_three = parts[:, D:].astype(bf16)
    adapt_ffn = product_rows(normed_two, grad_three)
    grad_normed_two = parts[:, :D] + product_back(grad_three, ffn_into)
    gain_two_grad = jnp.sum(grad_normed_two * unit_two, axis=0)
    grad_middle = cotangent.astype(f32) + norm_back(
        grad_normed_two, unit_two, inverse_two, gain_two
    )
    grad_branch = grad_middle.astype(bf16)
    grad_two = product_back(grad_branch, proj_from).astype(bf16)
    def scatter_weights(terms, order):
        return Scatter(terms.astype(bf16), core + order, ranking)

    out_jobs = [
        scatter_weights(terms, order)
        for terms, order in zip(
            (
                product_rows(
                    attn_rows, jnp.concatenate([grad_branch[:, :half], grad_two], axis=1)
                ),
                product_rows(attn_rows, grad_branch[:, half:]),
                adapt_ffn,
            ),
            (backs[0], backs[2], backs[3]),
        )
    ]
    grad_attn = to_heads(
        (
            product_back(grad_branch[:, :half], proj_one)
            + product_back(grad_branch[:, half:], proj_two)
            + product_back(grad_two, proj_into)
        ).astype(bf16)
    )
    _, grad_attn = advance(*out_jobs, beside=grad_attn)

    grad_queries, grad_keys, grad_values = [], 0.0, 0.0
    for i, query_rows in enumerate(query_parts):
        grad_rows = grad_attn[i * piece_rows : (i + 1) * piece_rows]
        shares = kept[i] if kept else shares_of(tie(query_rows, grad_rows))
        delta = jnp.sum(grad_rows.astype(f32) * attended_parts[i], axis=-1, keepdims=True)
        grad_shares = product_back(grad_rows, values_all)
        grad_scores = (shares * (grad_shares - delta)).astype(bf16)
        grad_queries.append(product(grad_scores, keys_all) * score_scale)
        grad_keys = grad_keys + product_rows(grad_scores, query_rows) * score_scale
        grad_values = grad_values + product_rows(shares.astype(bf16), grad_rows)
    grad_query = jnp.concatenate(grad_queries, axis=0)
    turned = rotate(grad_query.reshape(H, tokens, DH), cosine, -sine_part).astype(bf16)
    joined_q_grad = to_rows(turned.reshape(H * tokens, DH))
    query_jobs = [
        scatter_weights(product_rows(normed_one, rows), order)
        for rows, order in zip(
            (joined_q_grad[:, :half], joined_q_grad[:, half:]), (backs[0], backs[2])
        )
    ]
    _, (grad_keys, grad_values) = advance(
        *out_jobs, beside=(grad_keys.astype(bf16), grad_values.astype(bf16))
    )
    kv_jobs = [
        Scatter(grad_keys, ("head", low) + upper + mid, row_axes),
        Scatter(grad_values, mid + (low,) + upper + ("head",), row_axes),
    ]
    _, down_sum = advance(*kv_jobs, *out_jobs, beside=down_sum)
    gate_sum = scatter_units(tie(gate_terms, down_sum))
    for _ in range(steps - 2):
        advance(*kv_jobs, *out_jobs)
    advance(*kv_jobs, *query_jobs)
    keys_back, values_back = kv_jobs[0].result(), kv_jobs[1].result()
    joined_kv_grad = jnp.concatenate(
        [rotate(keys_back, cosine, -sine_part).astype(bf16), values_back.astype(bf16)], axis=1
    )
    grad_joined = jnp.concatenate([joined_q_grad, joined_kv_grad], axis=1)
    grad_one = product_back(grad_joined, qkv_from).astype(bf16)
    grad_normed_one = (
        product_back(joined_q_grad[:, :half], query_one)
        + product_back(joined_q_grad[:, half:], query_two)
        + product_back(joined_kv_grad, kv_full)
        + product_back(grad_one, qkv_into)
    )
    gain_one_grad = jnp.sum(grad_normed_one * unit_one, axis=0)
    stream_grad = grad_middle + norm_back(grad_normed_one, unit_one, inverse_one, gain_one)
    last = (
        product_rows(normed_one, jnp.concatenate([joined_kv_grad, grad_one], axis=1)).astype(bf16),
        jnp.concatenate(
            [
                product_rows(lowrank_one, grad_joined).astype(bf16),
                product_rows(lowrank_two, grad_branch).astype(bf16),
                expand_down.astype(bf16),
                gain_one_grad.reshape(R, -1).astype(bf16),
                gain_two_grad.reshape(R, -1).astype(bf16),
                jnp.zeros((R, 128 - 2 * gain_columns), bf16),
            ],
            axis=1,
        ),
    )
    _, (last, gate_sum) = advance(*query_jobs, beside=(last, gate_sum))
    up_sum = scatter_units(tie(up_terms, gate_sum))
    last_jobs = [scatter_weights(terms, order) for terms, order in zip(last, (backs[0], backs[2]))]
    for _ in range(steps - 1):
        arrived, _ = advance(*query_jobs, *last_jobs)
    sums = [value.astype(f32) for value in tie((down_sum, gate_sum, up_sum), arrived)]
    weights_grad = (
        sums[0][:, :D],
        sums[0][:, D:],
        jnp.stack([sums[1][:, :D], sums[2][:, :D]], axis=1),
        jnp.stack([sums[1][:, D:], sums[2][:, D:]], axis=1),
    )
    _, weights_grad = advance(*last_jobs, beside=weights_grad)
    downweight_grad, downadapt_grad, gateweight_grad, gateexpand_grad = weights_grad
    advance(*last_jobs)
    kv_grad, expand_grad = last_jobs[0].result(), last_jobs[1].result()
    gains_grad = expand_grad[:, qkv_columns + 2 * D :]
    n_gain = attn_gain.shape[0]
    return (
        result,
        stream_grad,
        gains_grad[:, :gain_columns].reshape(n_gain),
        jnp.concatenate([job.result() for job in query_jobs] + [kv_grad[:, : 2 * DH]], axis=1),
        kv_grad[:, 2 * DH : 2 * DH + R],
        expand_grad[:, :qkv_columns],
        jnp.concatenate([job.result()[:, :half] for job in out_jobs[:2]], axis=1),
        out_jobs[0].result()[:, half:],
        expand_grad[:, qkv_columns : qkv_columns + D],
        gains_grad[:, gain_columns : 2 * gain_columns].reshape(n_gain),
        gateweight_grad,
        out_jobs[2].result(),
        gateexpand_grad,
        downweight_grad,
        downadapt_grad,
        expand_grad[:, qkv_columns + D : qkv_columns + 2 * D],
        root_means,
    )


def solution(mesh):
    levels = mesh.shape["blk"].bit_length() - 1
    ranking = ("seq", "head") + tuple(f"blk{i}" for i in reversed(range(levels)))
    fine = jax.sharding.Mesh(mesh.devices.reshape((2,) * len(ranking)), ranking)
    rows = [P(ranking, *([None] * (rank - 1))) for rank in range(4)]
    in_specs = tuple(
        rows[rank] for rank in (2, 1, 2, 2, 2, 2, 2, 2, 1, 3, 2, 3, 2, 2, 2, 2)
    )
    out_specs = tuple(
        rows[rank] for rank in (2, 2, 1, 2, 2, 2, 2, 2, 2, 1, 3, 2, 3, 2, 2, 2)
    ) + (P(None, ranking),)
    return jax.shard_map(
        functools.partial(body, ranking),
        mesh=fine,
        in_specs=in_specs,
        out_specs=out_specs,
        check_vma=False,
    )
```

```python
import functools
import math

import jax
import jax.numpy as jnp
from jax import lax
from jax.experimental import pallas as pl
from jax.sharding import PartitionSpec as P

D = 2048
H = 8
DH = 256
R = 256


EPSILON = 1e-06
NEGATIVE = -1e30


def product(former, latter):
    return jnp.dot(former, latter, preferred_element_type=jnp.float32)


def product_back(former, latter):
    return lax.dot_general(
        former, latter, (((1,), (1,)), ((), ())), preferred_element_type=jnp.float32
    )


def product_rows(former, latter):
    return lax.dot_general(
        former, latter, (((0,), (0,)), ((), ())), preferred_element_type=jnp.float32
    )


def rope_tables(positions, full_width):
    half_width = full_width // 2
    rates = jnp.exp(
        jnp.arange(half_width, dtype=jnp.float32) * (-2.0 * math.log(10000.0) / full_width)
    )
    angles = positions.astype(jnp.float32)[:, None] * rates[None, :]
    return (jnp.cos(angles), jnp.sin(angles))


def rotate(values, cosine, sine_part):
    half_width = values.shape[-1] // 2
    former = values[..., :half_width]
    latter = values[..., half_width:]
    return jnp.concatenate(
        [former * cosine - latter * sine_part, latter * cosine + former * sine_part], axis=-1
    )


def unit_rows(values):
    inverse = lax.rsqrt(jnp.mean(values * values, axis=-1, keepdims=True) + EPSILON)
    return (values * inverse, inverse)


def norm_back(grad_in, scaled_rows, inverse, gain_row):
    weighted = grad_in * gain_row
    return inverse * (
        weighted - scaled_rows * jnp.mean(weighted * scaled_rows, axis=-1, keepdims=True)
    )


def root_mean(values):
    return jnp.sqrt(jnp.mean(values * values, axis=-1))


def shift(values, axes, mask):
    size = lax.axis_size(axes)
    return lax.ppermute(values, axes, [(i, i ^ mask) for i in range(size)])


def place(own, other, axis_name, position):
    first = lax.axis_index(axis_name) == 0
    return jnp.stack(
        [jnp.where(first, own, other), jnp.where(first, other, own)], axis=position
    )


class Gather:
    def __init__(self, shard, order, ranking):
        self.value, self.order, self.ranking = shard, list(order), ranking
        self.tail, self.done = shard.shape[1:], []

    def start(self):
        return shift(self.value, self.order[0], 1)

    def finish(self, other):
        name = self.order.pop(0)
        position = sum(self.ranking.index(d) < self.ranking.index(name) for d in self.done)
        self.value = place(self.value, other, name, position)
        self.done.append(name)

    def result(self):
        return self.value.reshape((-1,) + self.tail)


class Scatter:
    def __init__(self, terms, order, ranking):
        self.left = [name for name in ranking if name in order]
        self.order = list(order)
        rows = terms.shape[0] // 2 ** len(order)
        self.value = terms.reshape((2,) * len(order) + (rows,) + terms.shape[1:])

    def start(self):
        name = self.order[0]
        position, mine = self.left.index(name), lax.axis_index(name)
        sent = lax.dynamic_index_in_dim(self.value, 1 - mine, position, keepdims=False)
        return shift(sent, name, 1)

    def finish(self, other):
        name = self.order.pop(0)
        position, mine = self.left.index(name), lax.axis_index(name)
        kept = lax.dynamic_index_in_dim(self.value, mine, position, keepdims=False)
        self.value = kept.astype(jnp.float32) + other.astype(jnp.float32)
        if self.order:
            self.value = self.value.astype(jnp.bfloat16)
        self.left.remove(name)

    def result(self):
        return self.value


class ScatterNear(Scatter):
    def start(self):
        position = self.left.index(self.order[0])
        sent = lax.index_in_dim(self.value, 1, position, keepdims=False)
        return shift(sent, self.order[0], 1)

    def finish(self, other):
        name = self.order.pop(0)
        kept = lax.index_in_dim(self.value, 0, self.left.index(name), keepdims=False)
        self.value = kept.astype(jnp.float32) + other.astype(jnp.float32)
        if self.order:
            self.value = self.value.astype(jnp.bfloat16)
        self.left.remove(name)


def advance(*jobs, beside=()):
    arrived = [job.start() for job in jobs]
    if callable(beside):
        beside = beside(arrived[-1])
    arrived, beside = lax.optimization_barrier((arrived, beside))
    for job, other in zip(jobs, arrived):
        job.finish(other)
    return arrived, beside


def tie(values, *others):
    return lax.optimization_barrier((values, others))[0]


def pair_units(gate_sum, up_sum):
    units = gate_sum.shape[0]
    block = min(64, units)

    def kernel(gate_ref, up_ref, weight_ref, expand_ref):
        for k, ref in enumerate((gate_ref, up_ref)):
            terms = ref[...].astype(jnp.float32)
            weight_ref[:, k, :] = terms[:, :D]
            expand_ref[:, k, :] = terms[:, D:]

    return pl.pallas_call(
        kernel,
        grid=(units // block,),
        in_specs=[pl.BlockSpec((block, D + R), lambda i: (i, 0))] * 2,
        out_specs=[
            pl.BlockSpec((block, 2, D), lambda i: (i, 0, 0)),
            pl.BlockSpec((block, 2, R), lambda i: (i, 0, 0)),
        ],
        out_shape=[
            jax.ShapeDtypeStruct((units, 2, D), jnp.float32),
            jax.ShapeDtypeStruct((units, 2, R), jnp.float32),
        ],
        cost_estimate=pl.CostEstimate(
            flops=0, transcendentals=0, bytes_accessed=12 * units * (D + R)
        ),
    )(gate_sum, up_sum)


def body(
    ranking,
    stream,
    attn_gain,
    qkv_weight,
    qkv_adapt,
    qkv_expand,
    out_weight,
    out_adapt,
    out_expand,
    ffn_gain,
    gateup_weight,
    gateup_adapt,
    gateup_expand,
    down_weight,
    down_adapt,
    down_expand,
    cotangent,
):
    bf16 = jnp.bfloat16
    f32 = jnp.float32
    tokens = stream.shape[0]
    highs, low = ranking[2:-1], ranking[-1]
    row_axes, block_axes, unit_axes = ranking[1:], ranking[2:], ranking[:2]
    upper, mid, core = highs[:-1], highs[-1:], ("seq",)
    orders = (
        ("head",) + upper + (low,) + mid,
        ("head",) + mid + (low,) + upper,
        upper + ("head",) + mid + (low,),
        mid + ("head",) + upper + (low,),
    )
    steps = len(orders[0])
    backs = tuple(order[::-1] for order in orders)
    group = lax.axis_size(row_axes)
    planes = lax.axis_size(highs)
    plane = lax.axis_index(highs)
    side = lax.axis_index(low)
    own_pos = lax.axis_index(row_axes) * tokens + jnp.arange(tokens, dtype=jnp.int32)
    score_scale = DH ** (-0.5)
    half = H * DH // 2
    rank_rows = qkv_expand.shape[0]
    gain_columns = attn_gain.shape[0] // rank_rows

    from_row = jnp.concatenate(
        [
            qkv_expand,
            out_expand,
            down_expand,
            attn_gain.reshape(rank_rows, gain_columns),
            ffn_gain.reshape(rank_rows, gain_columns),
            jnp.zeros((rank_rows, 128 - 2 * gain_columns), bf16),
        ],
        axis=1,
    )
    jobs = [
        Gather(shard, order + core, ranking)
        for shard, order in zip(
            (
                jnp.concatenate([qkv_weight[:, 2 * half :], qkv_adapt], axis=1),
                from_row,
                qkv_weight[:, :half],
                qkv_weight[:, half : 2 * half],
            ),
            orders,
        )
    ]
    def gather_units(block):
        return lax.all_gather(block, unit_axes, axis=0, tiled=True)

    down_all = gather_units(jnp.concatenate([down_weight, down_adapt], axis=1))
    arrived, _ = advance(*jobs)
    pair_weight, pair_expand = tie((gateup_weight, gateup_expand), arrived)
    pairs = [
        jnp.concatenate([pair_weight[:, k], pair_expand[:, k]], axis=1) for k in range(2)
    ]
    arrived, pairs = advance(*jobs, beside=pairs)
    for _ in range(steps - 3):
        arrived, _ = advance(*jobs)
    gate_all = gather_units(tie(pairs[0], arrived))
    arrived, down_all = advance(*jobs, beside=down_all)
    advance(*jobs)
    kv_into, from_all, query_one, query_two = (job.result() for job in jobs)
    kv_full, qkv_into = kv_into[:, : 2 * DH], kv_into[:, 2 * DH :]
    qkv_columns = 2 * half + 2 * DH
    qkv_from = from_all[:, :qkv_columns]
    proj_from = from_all[:, qkv_columns : qkv_columns + D]
    down_from = from_all[:, qkv_columns + D : qkv_columns + 2 * D]
    gains = from_all[:, qkv_columns + 2 * D :]
    gain_one = gains[:, :gain_columns].reshape(D).astype(f32)
    gain_two = gains[:, gain_columns : 2 * gain_columns].reshape(D).astype(f32)

    residual = stream.astype(f32)
    unit_one, inverse_one = unit_rows(residual)
    normed_one = (unit_one * gain_one).astype(bf16)
    lowrank_one = product(normed_one, qkv_into).astype(bf16)
    joined_kv = product(normed_one, kv_full) + product(lowrank_one, qkv_from[:, 2 * half :])
    cosine, sine_part = rope_tables(own_pos, DH)
    keys = rotate(joined_kv[:, :DH], cosine, sine_part).astype(bf16)
    values = joined_kv[:, DH:].astype(bf16)
    joined_q = jnp.concatenate(
        [product(normed_one, query_one), product(normed_one, query_two)], axis=1
    ) + product(lowrank_one, qkv_from[:, : 2 * half])
    queries = (
        rotate(jnp.stack(jnp.split(joined_q, H, axis=1)), cosine, sine_part)
        .astype(bf16)
        .reshape(H * tokens, DH)
    )

    jobs = [
        Gather(shard, order, ranking)
        for shard, order in zip(
            (
                keys,
                values,
                jnp.concatenate([out_weight[:, :half], out_adapt], axis=1),
                jnp.concatenate([out_weight[:, half:], gateup_adapt], axis=1),
            ),
            (orders[1], orders[3], orders[0] + core, orders[2] + core),
        )
    ]
    arrived, (queries, gate_all) = advance(*jobs, beside=(queries, gate_all))
    up_all = gather_units(tie(pairs[1], gate_all))
    for _ in range(steps - 2):
        arrived, _ = advance(*jobs)
    arrived, up_all = advance(*jobs, beside=up_all)
    keys_all, values_all = jobs[0].result(), jobs[1].result()
    advance(*jobs[2:])
    out_one, out_two = jobs[2].result(), jobs[3].result()
    proj_one, proj_into = out_one[:, :half], out_one[:, half:]
    proj_two, ffn_into = out_two[:, :half], out_two[:, half:]

    def gather_near(rows):
        return [rows] + [shift(rows, highs, mask) for mask in range(1, planes)]

    def to_relative(rows):
        return jnp.concatenate(
            [
                lax.dynamic_slice_in_dim(
                    rows, ((plane ^ mask) * 2 + (side ^ far)) * tokens, tokens, 0
                )
                for far in range(2)
                for mask in range(planes)
            ],
            axis=0,
        )

    def to_absolute(rows):
        return jnp.concatenate(
            [
                lax.dynamic_slice_in_dim(
                    rows, ((side ^ far) * planes + (plane ^ mask)) * tokens, tokens, 0
                )
                for mask in range(planes)
                for far in range(2)
            ],
            axis=0,
        )

    key_pos = jnp.arange(group * tokens, dtype=jnp.int32)
    pieces = max(1, group * tokens // 2048)
    piece_rows = H * tokens // pieces
    visible = jnp.tile(key_pos[None, :] <= own_pos[:, None], (H // pieces, 1))

    def shares_of(query_rows):
        scores = jnp.where(
            visible, product_back(query_rows, keys_all) * score_scale, NEGATIVE
        )
        row_top = jnp.max(scores, axis=-1, keepdims=True)
        raised = jnp.where(visible, jnp.exp(scores - row_top), 0.0)
        return raised / jnp.sum(raised, axis=-1, keepdims=True)

    query_parts = jnp.split(queries, pieces, axis=0)
    kept, attended_parts = [], []
    for query_rows in query_parts:
        shares = shares_of(query_rows)
        attended_parts.append(product(shares.astype(bf16), values_all))
        if pieces == 1:
            kept.append(shares)

    def to_rows(parts):
        return jnp.concatenate(jnp.split(parts, H, axis=0), axis=1)

    def to_heads(rows):
        return jnp.concatenate(jnp.split(rows, H, axis=1), axis=0)

    attn_rows = to_rows(jnp.concatenate(attended_parts, axis=0).astype(bf16))
    lowrank_two = product(attn_rows, proj_into).astype(bf16)
    branch_attn = jnp.concatenate(
        [product(attn_rows, proj_one), product(attn_rows, proj_two)], axis=1
    ) + product(lowrank_two, proj_from)
    middle = residual + branch_attn
    unit_two, inverse_two = unit_rows(middle)
    normed_two = (unit_two * gain_two).astype(bf16)

    near = gather_near(normed_two)
    rows_group = jnp.concatenate(near + [shift(piece, low, 1) for piece in near], axis=0)
    back_all = lax.all_gather(
        tie(cotangent, near[1:], up_all), block_axes, axis=0, tiled=True
    )
    low_group = product(rows_group, ffn_into).astype(bf16)
    rows_joined = jnp.concatenate([rows_group, low_group], axis=1)
    gate = product_back(rows_joined, gate_all)
    up = product_back(rows_joined, up_all)
    hidden = (jax.nn.gelu(gate, approximate=True) * up).astype(bf16)
    out_terms = to_absolute(product(hidden, down_all).astype(bf16))
    mixed = lax.psum_scatter(
        tie(out_terms, back_all), block_axes, scatter_dimension=0, tiled=True
    )
    back_rows = tie(to_relative(back_all), out_terms)
    back_low = product_back(back_rows, down_from).astype(bf16)
    back_joined = jnp.concatenate([back_rows, back_low], axis=1)
    grad_hidden = product_back(back_joined, down_all)
    _, pullback = jax.vjp(lambda a, b: jax.nn.gelu(a, approximate=True) * b, gate, up)
    grad_gate, grad_up = (term.astype(bf16) for term in pullback(grad_hidden))

    row_terms = (product(grad_gate, gate_all) + product(grad_up, up_all)).astype(bf16)
    middle_column = row_terms.shape[1] // 2
    jobs = [
        ScatterNear(row_terms[:, :middle_column], (low,) + mid + upper, (low,) + highs),
        ScatterNear(row_terms[:, middle_column:], mid + upper + (low,), (low,) + highs),
    ]
    def scatter_units(terms):
        return lax.psum_scatter(terms, unit_axes, scatter_dimension=0, tiled=True)

    hidden_late, gate_late = tie((hidden, grad_gate), row_terms)
    work = (
        product_rows(hidden_late, back_joined).astype(bf16),
        product_rows(gate_late, rows_joined).astype(bf16),
    )
    arrived, (down_terms, gate_terms, mixed) = advance(*jobs, beside=(*work, mixed))
    down_sum = scatter_units(tie(down_terms, mixed))
    up_terms = product_rows(tie(grad_up, arrived), rows_joined).astype(bf16)
    _, up_terms = advance(*jobs, beside=up_terms)
    mixed = mixed.astype(f32)
    for _ in range(len(highs) - 1):
        advance(*jobs)
    parts = jnp.concatenate([job.result() for job in jobs], axis=1)

    lowrank_four = mixed[:, D:].astype(bf16)
    branch_ffn = mixed[:, :D] + product(lowrank_four, down_from)
    final = middle + branch_ffn
    result = final.astype(bf16)
    root_means = jnp.stack([root_mean(final), root_mean(branch_attn), root_mean(branch_ffn)])
    expand_down = product_rows(lowrank_four, cotangent)

    grad_three = parts[:, D:].astype(bf16)
    adapt_ffn = product_rows(normed_two, grad_three)
    grad_normed_two = parts[:, :D] + product_back(grad_three, ffn_into)
    gain_two_grad = jnp.sum(grad_normed_two * unit_two, axis=0)
    grad_middle = cotangent.astype(f32) + norm_back(
        grad_normed_two, unit_two, inverse_two, gain_two
    )
    grad_branch = grad_middle.astype(bf16)
    grad_two = product_back(grad_branch, proj_from).astype(bf16)
    def scatter_weights(terms, order):
        return Scatter(terms.astype(bf16), core + order, ranking)

    out_jobs = [
        scatter_weights(terms, order)
        for terms, order in zip(
            (
                product_rows(
                    attn_rows, jnp.concatenate([grad_branch[:, :half], grad_two], axis=1)
                ),
                product_rows(attn_rows, grad_branch[:, half:]),
                adapt_ffn,
            ),
            (backs[0], backs[2], backs[3]),
        )
    ]
    grad_attn = to_heads(
        (
            product_back(grad_branch[:, :half], proj_one)
            + product_back(grad_branch[:, half:], proj_two)
            + product_back(grad_two, proj_into)
        ).astype(bf16)
    )
    _, grad_attn = advance(*out_jobs, beside=grad_attn)

    scores_back, grad_keys, grad_values = [], 0.0, 0.0
    for i, query_rows in enumerate(query_parts):
        grad_rows = grad_attn[i * piece_rows : (i + 1) * piece_rows]
        shares = kept[i] if kept else shares_of(tie(query_rows, grad_rows))
        delta = jnp.sum(grad_rows.astype(f32) * attended_parts[i], axis=-1, keepdims=True)
        grad_shares = product_back(grad_rows, values_all)
        grad_scores = (shares * (grad_shares - delta)).astype(bf16)
        scores_back.append(grad_scores)
        grad_keys = grad_keys + product_rows(grad_scores, query_rows) * score_scale
        grad_values = grad_values + product_rows(shares.astype(bf16), grad_rows)
    _, (grad_keys, grad_values, down_sum) = advance(
        *out_jobs, beside=(grad_keys.astype(bf16), grad_values.astype(bf16), down_sum)
    )
    gate_sum = scatter_units(tie(gate_terms, down_sum))
    kv_jobs = [
        Scatter(grad_keys, ("head", low) + upper + mid, row_axes),
        Scatter(grad_values, mid + (low,) + upper + ("head",), row_axes),
    ]

    def query_back(seen):
        parts, lowrank, rows = tie((scores_back, lowrank_two, grad_branch), seen)
        grad_query = jnp.concatenate([product(part, keys_all) for part in parts], axis=0)
        turned = rotate(
            grad_query.reshape(H, tokens, DH) * score_scale, cosine, -sine_part
        ).astype(bf16)
        joined = to_rows(turned.reshape(H * tokens, DH))
        return (
            joined,
            product_rows(normed_one, joined[:, :half]).astype(bf16),
            product_rows(normed_one, joined[:, half:]).astype(bf16),
            product_rows(lowrank, rows).astype(bf16),
        )

    _, (joined_q_grad, *query_terms, out_expand_terms) = advance(
        *kv_jobs, *out_jobs, beside=query_back
    )
    query_jobs = [
        scatter_weights(terms, order)
        for terms, order in zip(query_terms, (backs[0], backs[2]))
    ]
    for _ in range(steps - 2):
        advance(*kv_jobs, *out_jobs)
    advance(*kv_jobs, *query_jobs)
    keys_back, values_back = kv_jobs[0].result(), kv_jobs[1].result()
    joined_kv_grad = jnp.concatenate(
        [rotate(keys_back, cosine, -sine_part).astype(bf16), values_back.astype(bf16)], axis=1
    )
    grad_joined = jnp.concatenate([joined_q_grad, joined_kv_grad], axis=1)
    grad_one = product_back(grad_joined, qkv_from).astype(bf16)
    grad_normed_one = (
        product_back(joined_q_grad[:, :half], query_one)
        + product_back(joined_q_grad[:, half:], query_two)
        + product_back(joined_kv_grad, kv_full)
        + product_back(grad_one, qkv_into)
    )
    gain_one_grad = jnp.sum(grad_normed_one * unit_one, axis=0)
    stream_grad = grad_middle + norm_back(grad_normed_one, unit_one, inverse_one, gain_one)
    last = (
        product_rows(normed_one, jnp.concatenate([joined_kv_grad, grad_one], axis=1)).astype(bf16),
        jnp.concatenate(
            [
                product_rows(lowrank_one, grad_joined).astype(bf16),
                out_expand_terms,
                expand_down.astype(bf16),
                gain_one_grad.reshape(R, -1).astype(bf16),
                gain_two_grad.reshape(R, -1).astype(bf16),
                jnp.zeros((R, 128 - 2 * gain_columns), bf16),
            ],
            axis=1,
        ),
    )
    _, (last, gate_sum) = advance(*query_jobs, beside=(last, gate_sum))
    up_sum = scatter_units(tie(up_terms, gate_sum))
    last_jobs = [scatter_weights(terms, order) for terms, order in zip(last, (backs[0], backs[2]))]
    for _ in range(steps - 1):
        arrived, _ = advance(*query_jobs, *last_jobs)
    arrived, _ = advance(*last_jobs)
    down_sum, gate_sum, up_sum = tie((down_sum, gate_sum, up_sum), arrived)
    downweight_grad, downadapt_grad = down_sum[:, :D].astype(f32), down_sum[:, D:].astype(f32)
    gateweight_grad, gateexpand_grad = pair_units(gate_sum, up_sum)
    advance(*last_jobs)
    kv_grad, expand_grad = last_jobs[0].result(), last_jobs[1].result()
    gains_grad = expand_grad[:, qkv_columns + 2 * D :]
    n_gain = attn_gain.shape[0]
    return (
        result,
        stream_grad,
        gains_grad[:, :gain_columns].reshape(n_gain),
        jnp.concatenate([job.result() for job in query_jobs] + [kv_grad[:, : 2 * DH]], axis=1),
        kv_grad[:, 2 * DH : 2 * DH + R],
        expand_grad[:, :qkv_columns],
        jnp.concatenate([job.result()[:, :half] for job in out_jobs[:2]], axis=1),
        out_jobs[0].result()[:, half:],
        expand_grad[:, qkv_columns : qkv_columns + D],
        gains_grad[:, gain_columns : 2 * gain_columns].reshape(n_gain),
        gateweight_grad,
        out_jobs[2].result(),
        gateexpand_grad,
        downweight_grad,
        downadapt_grad,
        expand_grad[:, qkv_columns + D : qkv_columns + 2 * D],
        root_means,
    )


def solution(mesh):
    levels = mesh.shape["blk"].bit_length() - 1
    ranking = ("seq", "head") + tuple(f"blk{i}" for i in reversed(range(levels)))
    fine = jax.sharding.Mesh(mesh.devices.reshape((2,) * len(ranking)), ranking)
    rows = [P(ranking, *([None] * (rank - 1))) for rank in range(4)]
    in_specs = tuple(
        rows[rank] for rank in (2, 1, 2, 2, 2, 2, 2, 2, 1, 3, 2, 3, 2, 2, 2, 2)
    )
    out_specs = tuple(
        rows[rank] for rank in (2, 2, 1, 2, 2, 2, 2, 2, 2, 1, 3, 2, 3, 2, 2, 2)
    ) + (P(None, ranking),)
    return jax.shard_map(
        functools.partial(body, ranking),
        mesh=fine,
        in_specs=in_specs,
        out_specs=out_specs,
        check_vma=False,
    )
```

```python
import functools
import math

import jax
import jax.numpy as jnp
from jax import lax
from jax.experimental import pallas as pl
from jax.sharding import PartitionSpec as P

D = 2048
H = 8
DH = 256
R = 256


EPSILON = 1e-06
NEGATIVE = -1e30


def product(former, latter):
    return jnp.dot(former, latter, preferred_element_type=jnp.float32)


def product_back(former, latter):
    return lax.dot_general(
        former, latter, (((1,), (1,)), ((), ())), preferred_element_type=jnp.float32
    )


def product_rows(former, latter):
    return lax.dot_general(
        former, latter, (((0,), (0,)), ((), ())), preferred_element_type=jnp.float32
    )


def rope_tables(positions, full_width):
    half_width = full_width // 2
    rates = jnp.exp(
        jnp.arange(half_width, dtype=jnp.float32) * (-2.0 * math.log(10000.0) / full_width)
    )
    angles = positions.astype(jnp.float32)[:, None] * rates[None, :]
    return (jnp.cos(angles), jnp.sin(angles))


def rotate(values, cosine, sine_part):
    half_width = values.shape[-1] // 2
    former = values[..., :half_width]
    latter = values[..., half_width:]
    return jnp.concatenate(
        [former * cosine - latter * sine_part, latter * cosine + former * sine_part], axis=-1
    )


def unit_rows(values):
    inverse = lax.rsqrt(jnp.mean(values * values, axis=-1, keepdims=True) + EPSILON)
    return (values * inverse, inverse)


def norm_back(grad_in, scaled_rows, inverse, gain_row):
    weighted = grad_in * gain_row
    return inverse * (
        weighted - scaled_rows * jnp.mean(weighted * scaled_rows, axis=-1, keepdims=True)
    )


def root_mean(values):
    return jnp.sqrt(jnp.mean(values * values, axis=-1))


def shift(values, axes, mask):
    size = lax.axis_size(axes)
    return lax.ppermute(values, axes, [(i, i ^ mask) for i in range(size)])


def place(own, other, axis_name, position):
    first = lax.axis_index(axis_name) == 0
    return jnp.stack(
        [jnp.where(first, own, other), jnp.where(first, other, own)], axis=position
    )


class Gather:
    def __init__(self, shard, order, ranking):
        self.value, self.order, self.ranking = shard, list(order), ranking
        self.tail, self.done = shard.shape[1:], []

    def start(self):
        return shift(self.value, self.order[0], 1)

    def finish(self, other):
        name = self.order.pop(0)
        position = sum(self.ranking.index(d) < self.ranking.index(name) for d in self.done)
        self.value = place(self.value, other, name, position)
        self.done.append(name)

    def result(self):
        return self.value.reshape((-1,) + self.tail)


class Scatter:
    def __init__(self, terms, order, ranking):
        self.left = [name for name in ranking if name in order]
        self.order = list(order)
        rows = terms.shape[0] // 2 ** len(order)
        self.value = terms.reshape((2,) * len(order) + (rows,) + terms.shape[1:])

    def start(self):
        name = self.order[0]
        position, mine = self.left.index(name), lax.axis_index(name)
        sent = lax.dynamic_index_in_dim(self.value, 1 - mine, position, keepdims=False)
        return shift(sent, name, 1)

    def finish(self, other):
        name = self.order.pop(0)
        position, mine = self.left.index(name), lax.axis_index(name)
        kept = lax.dynamic_index_in_dim(self.value, mine, position, keepdims=False)
        self.value = kept.astype(jnp.float32) + other.astype(jnp.float32)
        if self.order:
            self.value = self.value.astype(jnp.bfloat16)
        self.left.remove(name)

    def result(self):
        return self.value


class ScatterNear(Scatter):
    def start(self):
        position = self.left.index(self.order[0])
        sent = lax.index_in_dim(self.value, 1, position, keepdims=False)
        return shift(sent, self.order[0], 1)

    def finish(self, other):
        name = self.order.pop(0)
        kept = lax.index_in_dim(self.value, 0, self.left.index(name), keepdims=False)
        self.value = kept.astype(jnp.float32) + other.astype(jnp.float32)
        if self.order:
            self.value = self.value.astype(jnp.bfloat16)
        self.left.remove(name)


def advance(*jobs, beside=()):
    arrived = [job.start() for job in jobs]
    if callable(beside):
        beside = beside(arrived[-1])
    arrived, beside = lax.optimization_barrier((arrived, beside))
    for job, other in zip(jobs, arrived):
        job.finish(other)
    return arrived, beside


def tie(values, *others):
    return lax.optimization_barrier((values, others))[0]


def pair_units(gate_sum, up_sum):
    units = gate_sum.shape[0]
    block = min(64, units)

    def kernel(gate_ref, up_ref, weight_ref, expand_ref):
        for k, ref in enumerate((gate_ref, up_ref)):
            terms = ref[...].astype(jnp.float32)
            weight_ref[:, k, :] = terms[:, :D]
            expand_ref[:, k, :] = terms[:, D:]

    return pl.pallas_call(
        kernel,
        grid=(units // block,),
        in_specs=[pl.BlockSpec((block, D + R), lambda i: (i, 0))] * 2,
        out_specs=[
            pl.BlockSpec((block, 2, D), lambda i: (i, 0, 0)),
            pl.BlockSpec((block, 2, R), lambda i: (i, 0, 0)),
        ],
        out_shape=[
            jax.ShapeDtypeStruct((units, 2, D), jnp.float32),
            jax.ShapeDtypeStruct((units, 2, R), jnp.float32),
        ],
        cost_estimate=pl.CostEstimate(
            flops=0, transcendentals=0, bytes_accessed=12 * units * (D + R)
        ),
    )(gate_sum, up_sum)


def body(
    ranking,
    stream,
    attn_gain,
    qkv_weight,
    qkv_adapt,
    qkv_expand,
    out_weight,
    out_adapt,
    out_expand,
    ffn_gain,
    gateup_weight,
    gateup_adapt,
    gateup_expand,
    down_weight,
    down_adapt,
    down_expand,
    cotangent,
):
    bf16 = jnp.bfloat16
    f32 = jnp.float32
    tokens = stream.shape[0]
    highs, low = ranking[2:-1], ranking[-1]
    row_axes, block_axes, unit_axes = ranking[1:], ranking[2:], ranking[:2]
    upper, mid, core = highs[:-1], highs[-1:], ("seq",)
    orders = (
        ("head",) + upper + (low,) + mid,
        ("head",) + mid + (low,) + upper,
        upper + ("head",) + mid + (low,),
        mid + ("head",) + upper + (low,),
    )
    steps = len(orders[0])
    backs = tuple(order[::-1] for order in orders)
    group = lax.axis_size(row_axes)
    planes = lax.axis_size(highs)
    plane = lax.axis_index(highs)
    side = lax.axis_index(low)
    own_pos = lax.axis_index(row_axes) * tokens + jnp.arange(tokens, dtype=jnp.int32)
    score_scale = DH ** (-0.5)
    half = H * DH // 2
    rank_rows = qkv_expand.shape[0]
    gain_columns = attn_gain.shape[0] // rank_rows

    from_row = jnp.concatenate(
        [
            qkv_expand,
            out_expand,
            down_expand,
            attn_gain.reshape(rank_rows, gain_columns),
            ffn_gain.reshape(rank_rows, gain_columns),
            jnp.zeros((rank_rows, 128 - 2 * gain_columns), bf16),
        ],
        axis=1,
    )
    jobs = [
        Gather(shard, order + core, ranking)
        for shard, order in zip(
            (
                jnp.concatenate([qkv_weight[:, 2 * half :], qkv_adapt], axis=1),
                from_row,
                qkv_weight[:, :half],
                qkv_weight[:, half : 2 * half],
            ),
            orders,
        )
    ]
    def gather_units(block):
        return lax.all_gather(block, unit_axes, axis=0, tiled=True)

    arrived, _ = advance(*jobs)
    down_all = gather_units(
        jnp.concatenate(tie((down_weight, down_adapt), arrived[0]), axis=1)
    )
    pair_weight, pair_expand = tie((gateup_weight, gateup_expand), arrived)
    pairs = [
        jnp.concatenate([pair_weight[:, k], pair_expand[:, k]], axis=1) for k in range(2)
    ]
    arrived, pairs = advance(*jobs, beside=pairs)
    for _ in range(steps - 3):
        arrived, _ = advance(*jobs)
    gate_all = gather_units(tie(pairs[0], arrived))
    arrived, down_all = advance(*jobs, beside=down_all)
    advance(*jobs[:2])
    advance(*jobs[2:])
    kv_into, from_all, query_one, query_two = (job.result() for job in jobs)
    kv_full, qkv_into = kv_into[:, : 2 * DH], kv_into[:, 2 * DH :]
    qkv_columns = 2 * half + 2 * DH
    qkv_from = from_all[:, :qkv_columns]
    proj_from = from_all[:, qkv_columns : qkv_columns + D]
    down_from = from_all[:, qkv_columns + D : qkv_columns + 2 * D]
    gains = from_all[:, qkv_columns + 2 * D :]
    gain_one = gains[:, :gain_columns].reshape(D).astype(f32)
    gain_two = gains[:, gain_columns : 2 * gain_columns].reshape(D).astype(f32)

    residual = stream.astype(f32)
    unit_one, inverse_one = unit_rows(residual)
    normed_one = (unit_one * gain_one).astype(bf16)
    lowrank_one = product(normed_one, qkv_into).astype(bf16)
    joined_kv = product(normed_one, kv_full) + product(lowrank_one, qkv_from[:, 2 * half :])
    cosine, sine_part = rope_tables(own_pos, DH)
    keys = rotate(joined_kv[:, :DH], cosine, sine_part).astype(bf16)
    values = joined_kv[:, DH:].astype(bf16)
    joined_q = jnp.concatenate(
        [product(normed_one, query_one), product(normed_one, query_two)], axis=1
    ) + product(lowrank_one, qkv_from[:, : 2 * half])
    queries = (
        rotate(jnp.stack(jnp.split(joined_q, H, axis=1)), cosine, sine_part)
        .astype(bf16)
        .reshape(H * tokens, DH)
    )

    jobs = [
        Gather(shard, order, ranking)
        for shard, order in zip(
            (
                keys,
                values,
                jnp.concatenate([out_weight[:, :half], out_adapt], axis=1),
                jnp.concatenate([out_weight[:, half:], gateup_adapt], axis=1),
            ),
            (orders[1], orders[3], orders[0] + core, orders[2] + core),
        )
    ]
    arrived, (queries, gate_all) = advance(*jobs, beside=(queries, gate_all))
    up_all = gather_units(tie(pairs[1], gate_all))
    for _ in range(steps - 2):
        arrived, _ = advance(*jobs)
    arrived, up_all = advance(*jobs, beside=up_all)
    keys_all, values_all = jobs[0].result(), jobs[1].result()
    advance(*jobs[2:])
    out_one, out_two = jobs[2].result(), jobs[3].result()
    proj_one, proj_into = out_one[:, :half], out_one[:, half:]
    proj_two, ffn_into = out_two[:, :half], out_two[:, half:]

    def gather_near(rows):
        return [rows] + [shift(rows, highs, mask) for mask in range(1, planes)]

    def to_relative(rows):
        return jnp.concatenate(
            [
                lax.dynamic_slice_in_dim(
                    rows, ((plane ^ mask) * 2 + (side ^ far)) * tokens, tokens, 0
                )
                for far in range(2)
                for mask in range(planes)
            ],
            axis=0,
        )

    def to_absolute(rows):
        return jnp.concatenate(
            [
                lax.dynamic_slice_in_dim(
                    rows, ((side ^ far) * planes + (plane ^ mask)) * tokens, tokens, 0
                )
                for mask in range(planes)
                for far in range(2)
            ],
            axis=0,
        )

    key_pos = jnp.arange(group * tokens, dtype=jnp.int32)
    pieces = max(1, group * tokens // 2048)
    piece_rows = H * tokens // pieces
    visible = jnp.tile(key_pos[None, :] <= own_pos[:, None], (H // pieces, 1))

    def shares_of(query_rows):
        scores = jnp.where(
            visible, product_back(query_rows, keys_all) * score_scale, NEGATIVE
        )
        row_top = jnp.max(scores, axis=-1, keepdims=True)
        raised = jnp.where(visible, jnp.exp(scores - row_top), 0.0)
        return raised / jnp.sum(raised, axis=-1, keepdims=True)

    query_parts = jnp.split(queries, pieces, axis=0)
    kept, attended_parts = [], []
    for query_rows in query_parts:
        shares = shares_of(query_rows)
        attended_parts.append(product(shares.astype(bf16), values_all))
        if pieces == 1:
            kept.append(shares)

    def to_rows(parts):
        return jnp.concatenate(jnp.split(parts, H, axis=0), axis=1)

    def to_heads(rows):
        return jnp.concatenate(jnp.split(rows, H, axis=1), axis=0)

    attn_rows = to_rows(jnp.concatenate(attended_parts, axis=0).astype(bf16))
    lowrank_two = product(attn_rows, proj_into).astype(bf16)
    branch_attn = jnp.concatenate(
        [product(attn_rows, proj_one), product(attn_rows, proj_two)], axis=1
    ) + product(lowrank_two, proj_from)
    middle = residual + branch_attn
    unit_two, inverse_two = unit_rows(middle)
    normed_two = (unit_two * gain_two).astype(bf16)

    near = gather_near(normed_two)
    rows_group = jnp.concatenate(near + [shift(piece, low, 1) for piece in near], axis=0)
    back_all = lax.all_gather(
        tie(cotangent, near[1:], up_all), block_axes, axis=0, tiled=True
    )
    low_group = product(rows_group, ffn_into).astype(bf16)
    rows_joined = jnp.concatenate([rows_group, low_group], axis=1)
    gate = product_back(rows_joined, gate_all)
    up = product_back(rows_joined, up_all)
    hidden = (jax.nn.gelu(gate, approximate=True) * up).astype(bf16)
    out_terms = to_absolute(product(hidden, down_all).astype(bf16))
    mixed = lax.psum_scatter(
        tie(out_terms, back_all), block_axes, scatter_dimension=0, tiled=True
    )
    back_rows = tie(to_relative(back_all), out_terms)
    back_low = product_back(back_rows, down_from).astype(bf16)
    back_joined = jnp.concatenate([back_rows, back_low], axis=1)
    grad_hidden = product_back(back_joined, down_all)
    _, pullback = jax.vjp(lambda a, b: jax.nn.gelu(a, approximate=True) * b, gate, up)
    grad_gate, grad_up = (term.astype(bf16) for term in pullback(grad_hidden))

    row_terms = (product(grad_gate, gate_all) + product(grad_up, up_all)).astype(bf16)
    middle_column = row_terms.shape[1] // 2
    jobs = [
        ScatterNear(row_terms[:, :middle_column], (low,) + mid + upper, (low,) + highs),
        ScatterNear(row_terms[:, middle_column:], mid + upper + (low,), (low,) + highs),
    ]
    def scatter_units(terms):
        return lax.psum_scatter(terms, unit_axes, scatter_dimension=0, tiled=True)

    hidden_late, gate_late = tie((hidden, grad_gate), row_terms)
    work = (
        product_rows(hidden_late, back_joined).astype(bf16),
        product_rows(gate_late, rows_joined).astype(bf16),
    )
    arrived, (down_terms, gate_terms, mixed) = advance(*jobs, beside=(*work, mixed))
    down_sum = scatter_units(tie(down_terms, mixed))
    up_terms = product_rows(tie(grad_up, arrived), rows_joined).astype(bf16)
    _, up_terms = advance(*jobs, beside=up_terms)
    mixed = mixed.astype(f32)
    for _ in range(len(highs) - 1):
        advance(*jobs)
    parts = jnp.concatenate([job.result() for job in jobs], axis=1)

    lowrank_four = mixed[:, D:].astype(bf16)
    branch_ffn = mixed[:, :D] + product(lowrank_four, down_from)
    final = middle + branch_ffn
    result = final.astype(bf16)
    root_means = jnp.stack([root_mean(final), root_mean(branch_attn), root_mean(branch_ffn)])
    expand_down = product_rows(lowrank_four, cotangent)

    grad_three = parts[:, D:].astype(bf16)
    adapt_ffn = product_rows(normed_two, grad_three)
    grad_normed_two = parts[:, :D] + product_back(grad_three, ffn_into)
    gain_two_grad = jnp.sum(grad_normed_two * unit_two, axis=0)
    grad_middle = cotangent.astype(f32) + norm_back(
        grad_normed_two, unit_two, inverse_two, gain_two
    )
    grad_branch = grad_middle.astype(bf16)
    grad_two = product_back(grad_branch, proj_from).astype(bf16)
    def scatter_weights(terms, order):
        return Scatter(terms.astype(bf16), core + order, ranking)

    out_jobs = [
        scatter_weights(terms, order)
        for terms, order in zip(
            (
                product_rows(
                    attn_rows, jnp.concatenate([grad_branch[:, :half], grad_two], axis=1)
                ),
                product_rows(attn_rows, grad_branch[:, half:]),
                adapt_ffn,
            ),
            (backs[0], backs[2], backs[3]),
        )
    ]
    grad_attn = to_heads(
        (
            product_back(grad_branch[:, :half], proj_one)
            + product_back(grad_branch[:, half:], proj_two)
            + product_back(grad_two, proj_into)
        ).astype(bf16)
    )
    _, grad_attn = advance(*out_jobs, beside=grad_attn)

    scores_back, grad_keys, grad_values = [], 0.0, 0.0
    for i, query_rows in enumerate(query_parts):
        grad_rows = grad_attn[i * piece_rows : (i + 1) * piece_rows]
        shares = kept[i] if kept else shares_of(tie(query_rows, grad_rows))
        delta = jnp.sum(grad_rows.astype(f32) * attended_parts[i], axis=-1, keepdims=True)
        grad_shares = product_back(grad_rows, values_all)
        grad_scores = (shares * (grad_shares - delta)).astype(bf16)
        scores_back.append(grad_scores)
        grad_keys = grad_keys + product_rows(grad_scores, query_rows) * score_scale
        grad_values = grad_values + product_rows(shares.astype(bf16), grad_rows)
    _, (grad_keys, grad_values, down_sum) = advance(
        *out_jobs, beside=(grad_keys.astype(bf16), grad_values.astype(bf16), down_sum)
    )
    gate_sum = scatter_units(tie(gate_terms, down_sum))
    kv_jobs = [
        Scatter(grad_keys, ("head", low) + upper + mid, row_axes),
        Scatter(grad_values, mid + (low,) + upper + ("head",), row_axes),
    ]

    def query_back(seen):
        parts, lowrank, rows = tie((scores_back, lowrank_two, grad_branch), seen)
        grad_query = jnp.concatenate([product(part, keys_all) for part in parts], axis=0)
        turned = rotate(
            grad_query.reshape(H, tokens, DH) * score_scale, cosine, -sine_part
        ).astype(bf16)
        joined = to_rows(turned.reshape(H * tokens, DH))
        return (
            joined,
            product_rows(normed_one, joined[:, :half]).astype(bf16),
            product_rows(normed_one, joined[:, half:]).astype(bf16),
            product_rows(lowrank, rows).astype(bf16),
        )

    _, (joined_q_grad, *query_terms, out_expand_terms) = advance(
        *kv_jobs, *out_jobs, beside=query_back
    )
    query_jobs = [
        scatter_weights(terms, order)
        for terms, order in zip(query_terms, (backs[0], backs[2]))
    ]
    for _ in range(steps - 2):
        advance(*kv_jobs, *out_jobs)
    advance(*kv_jobs, *query_jobs)
    keys_back, values_back = kv_jobs[0].result(), kv_jobs[1].result()
    joined_kv_grad = jnp.concatenate(
        [rotate(keys_back, cosine, -sine_part).astype(bf16), values_back.astype(bf16)], axis=1
    )
    grad_joined = jnp.concatenate([joined_q_grad, joined_kv_grad], axis=1)
    grad_one = product_back(grad_joined, qkv_from).astype(bf16)
    grad_normed_one = (
        product_back(joined_q_grad[:, :half], query_one)
        + product_back(joined_q_grad[:, half:], query_two)
        + product_back(joined_kv_grad, kv_full)
        + product_back(grad_one, qkv_into)
    )
    gain_one_grad = jnp.sum(grad_normed_one * unit_one, axis=0)
    stream_grad = grad_middle + norm_back(grad_normed_one, unit_one, inverse_one, gain_one)
    last = (
        product_rows(normed_one, jnp.concatenate([joined_kv_grad, grad_one], axis=1)).astype(bf16),
        jnp.concatenate(
            [
                product_rows(lowrank_one, grad_joined).astype(bf16),
                out_expand_terms,
                expand_down.astype(bf16),
                gain_one_grad.reshape(R, -1).astype(bf16),
                gain_two_grad.reshape(R, -1).astype(bf16),
                jnp.zeros((R, 128 - 2 * gain_columns), bf16),
            ],
            axis=1,
        ),
    )
    _, (last, gate_sum) = advance(*query_jobs, beside=(last, gate_sum))
    up_sum = scatter_units(tie(up_terms, gate_sum))
    last_jobs = [scatter_weights(terms, order) for terms, order in zip(last, (backs[0], backs[2]))]
    for _ in range(steps - 1):
        arrived, _ = advance(*query_jobs, *last_jobs)
    arrived, _ = advance(*last_jobs)
    down_sum, gate_sum, up_sum = tie((down_sum, gate_sum, up_sum), arrived)
    downweight_grad, downadapt_grad = down_sum[:, :D].astype(f32), down_sum[:, D:].astype(f32)
    gateweight_grad, gateexpand_grad = pair_units(gate_sum, up_sum)
    advance(*last_jobs)
    kv_grad, expand_grad = last_jobs[0].result(), last_jobs[1].result()
    gains_grad = expand_grad[:, qkv_columns + 2 * D :]
    n_gain = attn_gain.shape[0]
    return (
        result,
        stream_grad,
        gains_grad[:, :gain_columns].reshape(n_gain),
        jnp.concatenate([job.result() for job in query_jobs] + [kv_grad[:, : 2 * DH]], axis=1),
        kv_grad[:, 2 * DH : 2 * DH + R],
        expand_grad[:, :qkv_columns],
        jnp.concatenate([job.result()[:, :half] for job in out_jobs[:2]], axis=1),
        out_jobs[0].result()[:, half:],
        expand_grad[:, qkv_columns : qkv_columns + D],
        gains_grad[:, gain_columns : 2 * gain_columns].reshape(n_gain),
        gateweight_grad,
        out_jobs[2].result(),
        gateexpand_grad,
        downweight_grad,
        downadapt_grad,
        expand_grad[:, qkv_columns + D : qkv_columns + 2 * D],
        root_means,
    )


def solution(mesh):
    levels = mesh.shape["blk"].bit_length() - 1
    ranking = ("seq", "head") + tuple(f"blk{i}" for i in reversed(range(levels)))
    fine = jax.sharding.Mesh(mesh.devices.reshape((2,) * len(ranking)), ranking)
    rows = [P(ranking, *([None] * (rank - 1))) for rank in range(4)]
    in_specs = tuple(
        rows[rank] for rank in (2, 1, 2, 2, 2, 2, 2, 2, 1, 3, 2, 3, 2, 2, 2, 2)
    )
    out_specs = tuple(
        rows[rank] for rank in (2, 2, 1, 2, 2, 2, 2, 2, 2, 1, 3, 2, 3, 2, 2, 2)
    ) + (P(None, ranking),)
    return jax.shard_map(
        functools.partial(body, ranking),
        mesh=fine,
        in_specs=in_specs,
        out_specs=out_specs,
        check_vma=False,
    )
```

```python
import functools
import math

import jax
import jax.numpy as jnp
from jax import lax
from jax.experimental import pallas as pl
from jax.sharding import PartitionSpec as P

D = 2048
H = 8
DH = 256
R = 256


EPSILON = 1e-06
NEGATIVE = -1e30


def product(former, latter):
    return jnp.dot(former, latter, preferred_element_type=jnp.float32)


def product_back(former, latter):
    return lax.dot_general(
        former, latter, (((1,), (1,)), ((), ())), preferred_element_type=jnp.float32
    )


def product_rows(former, latter):
    return lax.dot_general(
        former, latter, (((0,), (0,)), ((), ())), preferred_element_type=jnp.float32
    )


def rope_tables(positions, full_width):
    half_width = full_width // 2
    rates = jnp.exp(
        jnp.arange(half_width, dtype=jnp.float32) * (-2.0 * math.log(10000.0) / full_width)
    )
    angles = positions.astype(jnp.float32)[:, None] * rates[None, :]
    return (jnp.cos(angles), jnp.sin(angles))


def rotate(values, cosine, sine_part):
    half_width = values.shape[-1] // 2
    former = values[..., :half_width]
    latter = values[..., half_width:]
    return jnp.concatenate(
        [former * cosine - latter * sine_part, latter * cosine + former * sine_part], axis=-1
    )


def unit_rows(values):
    inverse = lax.rsqrt(jnp.mean(values * values, axis=-1, keepdims=True) + EPSILON)
    return (values * inverse, inverse)


def norm_back(grad_in, scaled_rows, inverse, gain_row):
    weighted = grad_in * gain_row
    return inverse * (
        weighted - scaled_rows * jnp.mean(weighted * scaled_rows, axis=-1, keepdims=True)
    )


def root_mean(values):
    return jnp.sqrt(jnp.mean(values * values, axis=-1))


def shift(values, axes, mask):
    size = lax.axis_size(axes)
    return lax.ppermute(values, axes, [(i, i ^ mask) for i in range(size)])


def place(own, other, axis_name, position):
    first = lax.axis_index(axis_name) == 0
    return jnp.stack(
        [jnp.where(first, own, other), jnp.where(first, other, own)], axis=position
    )


class Gather:
    def __init__(self, shard, order, ranking):
        self.value, self.order, self.ranking = shard, list(order), ranking
        self.tail, self.done = shard.shape[1:], []

    def start(self):
        return shift(self.value, self.order[0], 1)

    def finish(self, other):
        name = self.order.pop(0)
        position = sum(self.ranking.index(d) < self.ranking.index(name) for d in self.done)
        self.value = place(self.value, other, name, position)
        self.done.append(name)

    def result(self):
        return self.value.reshape((-1,) + self.tail)


class Scatter:
    def __init__(self, terms, order, ranking):
        self.left = [name for name in ranking if name in order]
        self.order = list(order)
        rows = terms.shape[0] // 2 ** len(order)
        self.value = terms.reshape((2,) * len(order) + (rows,) + terms.shape[1:])

    def start(self):
        name = self.order[0]
        position, mine = self.left.index(name), lax.axis_index(name)
        sent = lax.dynamic_index_in_dim(self.value, 1 - mine, position, keepdims=False)
        return shift(sent, name, 1)

    def finish(self, other):
        name = self.order.pop(0)
        position, mine = self.left.index(name), lax.axis_index(name)
        kept = lax.dynamic_index_in_dim(self.value, mine, position, keepdims=False)
        self.value = kept.astype(jnp.float32) + other.astype(jnp.float32)
        if self.order:
            self.value = self.value.astype(jnp.bfloat16)
        self.left.remove(name)

    def result(self):
        return self.value


class ScatterNear(Scatter):
    def start(self):
        position = self.left.index(self.order[0])
        sent = lax.index_in_dim(self.value, 1, position, keepdims=False)
        return shift(sent, self.order[0], 1)

    def finish(self, other):
        name = self.order.pop(0)
        kept = lax.index_in_dim(self.value, 0, self.left.index(name), keepdims=False)
        self.value = kept.astype(jnp.float32) + other.astype(jnp.float32)
        if self.order:
            self.value = self.value.astype(jnp.bfloat16)
        self.left.remove(name)


def advance(*jobs, beside=()):
    arrived = [job.start() for job in jobs]
    if callable(beside):
        beside = beside(arrived[-1])
    arrived, beside = lax.optimization_barrier((arrived, beside))
    for job, other in zip(jobs, arrived):
        job.finish(other)
    return arrived, beside


def tie(values, *others):
    return lax.optimization_barrier((values, others))[0]


def pair_units(gate_sum, up_sum):
    units = gate_sum.shape[0]
    block = min(64, units)

    def kernel(gate_ref, up_ref, weight_ref, expand_ref):
        for k, ref in enumerate((gate_ref, up_ref)):
            terms = ref[...].astype(jnp.float32)
            weight_ref[:, k, :] = terms[:, :D]
            expand_ref[:, k, :] = terms[:, D:]

    return pl.pallas_call(
        kernel,
        grid=(units // block,),
        in_specs=[pl.BlockSpec((block, D + R), lambda i: (i, 0))] * 2,
        out_specs=[
            pl.BlockSpec((block, 2, D), lambda i: (i, 0, 0)),
            pl.BlockSpec((block, 2, R), lambda i: (i, 0, 0)),
        ],
        out_shape=[
            jax.ShapeDtypeStruct((units, 2, D), jnp.float32),
            jax.ShapeDtypeStruct((units, 2, R), jnp.float32),
        ],
        cost_estimate=pl.CostEstimate(
            flops=0, transcendentals=0, bytes_accessed=12 * units * (D + R)
        ),
    )(gate_sum, up_sum)


def body(
    ranking,
    stream,
    attn_gain,
    qkv_weight,
    qkv_adapt,
    qkv_expand,
    out_weight,
    out_adapt,
    out_expand,
    ffn_gain,
    gateup_weight,
    gateup_adapt,
    gateup_expand,
    down_weight,
    down_adapt,
    down_expand,
    cotangent,
):
    bf16 = jnp.bfloat16
    f32 = jnp.float32
    tokens = stream.shape[0]
    highs, low = ranking[2:-1], ranking[-1]
    row_axes, block_axes, unit_axes = ranking[1:], ranking[2:], ranking[:2]
    upper, mid, core = highs[:-1], highs[-1:], ("seq",)
    orders = (
        ("head",) + upper + (low,) + mid,
        ("head",) + mid + (low,) + upper,
        upper + ("head",) + mid + (low,),
        mid + ("head",) + upper + (low,),
    )
    steps = len(orders[0])
    backs = tuple(order[::-1] for order in orders)
    group = lax.axis_size(row_axes)
    planes = lax.axis_size(highs)
    plane = lax.axis_index(highs)
    side = lax.axis_index(low)
    own_pos = lax.axis_index(row_axes) * tokens + jnp.arange(tokens, dtype=jnp.int32)
    score_scale = DH ** (-0.5)
    half = H * DH // 2
    rank_rows = qkv_expand.shape[0]
    gain_columns = attn_gain.shape[0] // rank_rows

    from_row = jnp.concatenate(
        [
            qkv_expand,
            out_expand,
            down_expand,
            attn_gain.reshape(rank_rows, gain_columns),
            ffn_gain.reshape(rank_rows, gain_columns),
            jnp.zeros((rank_rows, 128 - 2 * gain_columns), bf16),
        ],
        axis=1,
    )
    jobs = [
        Gather(shard, order + core, ranking)
        for shard, order in zip(
            (
                jnp.concatenate([qkv_weight[:, 2 * half :], qkv_adapt], axis=1),
                from_row,
                qkv_weight[:, :half],
                qkv_weight[:, half : 2 * half],
            ),
            orders,
        )
    ]
    def gather_units(block):
        return lax.all_gather(block, unit_axes, axis=0, tiled=True)

    arrived, _ = advance(*jobs)
    down_all = gather_units(
        jnp.concatenate(tie((down_weight, down_adapt), arrived[0]), axis=1)
    )
    pair_weight, pair_expand = tie((gateup_weight, gateup_expand), arrived)
    pairs = [
        jnp.concatenate([pair_weight[:, k], pair_expand[:, k]], axis=1) for k in range(2)
    ]
    arrived, pairs = advance(*jobs, beside=pairs)
    for _ in range(steps - 3):
        arrived, _ = advance(*jobs)
    gate_all = gather_units(tie(pairs[0], arrived))
    arrived, down_all = advance(*jobs, beside=down_all)
    advance(*jobs[:2])
    advance(*jobs[2:])
    kv_into, from_all, query_one, query_two = (job.result() for job in jobs)
    kv_full, qkv_into = kv_into[:, : 2 * DH], kv_into[:, 2 * DH :]
    qkv_columns = 2 * half + 2 * DH
    qkv_from = from_all[:, :qkv_columns]
    proj_from = from_all[:, qkv_columns : qkv_columns + D]
    down_from = from_all[:, qkv_columns + D : qkv_columns + 2 * D]
    gains = from_all[:, qkv_columns + 2 * D :]
    gain_one = gains[:, :gain_columns].reshape(D).astype(f32)
    gain_two = gains[:, gain_columns : 2 * gain_columns].reshape(D).astype(f32)

    residual = stream.astype(f32)
    unit_one, inverse_one = unit_rows(residual)
    normed_one = (unit_one * gain_one).astype(bf16)
    lowrank_one = product(normed_one, qkv_into).astype(bf16)
    joined_kv = product(normed_one, kv_full) + product(lowrank_one, qkv_from[:, 2 * half :])
    cosine, sine_part = rope_tables(own_pos, DH)
    keys = rotate(joined_kv[:, :DH], cosine, sine_part).astype(bf16)
    values = joined_kv[:, DH:].astype(bf16)
    joined_q = jnp.concatenate(
        [product(normed_one, query_one), product(normed_one, query_two)], axis=1
    ) + product(lowrank_one, qkv_from[:, : 2 * half])
    queries = (
        rotate(jnp.stack(jnp.split(joined_q, H, axis=1)), cosine, sine_part)
        .astype(bf16)
        .reshape(H * tokens, DH)
    )

    jobs = [
        Gather(shard, order, ranking)
        for shard, order in zip(
            (
                keys,
                values,
                jnp.concatenate([out_weight[:, :half], out_adapt], axis=1),
                jnp.concatenate([out_weight[:, half:], gateup_adapt], axis=1),
            ),
            (orders[1], orders[3], orders[0] + core, orders[2] + core),
        )
    ]
    arrived, (queries, gate_all) = advance(*jobs, beside=(queries, gate_all))
    up_all = gather_units(tie(pairs[1], gate_all))
    for _ in range(steps - 2):
        arrived, _ = advance(*jobs)
    arrived, up_all = advance(*jobs, beside=up_all)
    keys_all, values_all = jobs[0].result(), jobs[1].result()
    advance(*jobs[2:])
    out_one, out_two = jobs[2].result(), jobs[3].result()
    proj_one, proj_into = out_one[:, :half], out_one[:, half:]
    proj_two, ffn_into = out_two[:, :half], out_two[:, half:]

    def gather_near(rows):
        return [rows] + [shift(rows, highs, mask) for mask in range(1, planes)]

    def to_relative(rows):
        return jnp.concatenate(
            [
                lax.dynamic_slice_in_dim(
                    rows, ((plane ^ mask) * 2 + (side ^ far)) * tokens, tokens, 0
                )
                for far in range(2)
                for mask in range(planes)
            ],
            axis=0,
        )

    def to_absolute(rows):
        return jnp.concatenate(
            [
                lax.dynamic_slice_in_dim(
                    rows, ((side ^ far) * planes + (plane ^ mask)) * tokens, tokens, 0
                )
                for mask in range(planes)
                for far in range(2)
            ],
            axis=0,
        )

    key_pos = jnp.arange(group * tokens, dtype=jnp.int32)
    pieces = max(1, group * tokens // 2048)
    piece_rows = H * tokens // pieces
    visible = jnp.tile(key_pos[None, :] <= own_pos[:, None], (H // pieces, 1))

    def shares_of(query_rows):
        scores = jnp.where(
            visible, product_back(query_rows, keys_all) * score_scale, NEGATIVE
        )
        row_top = jnp.max(scores, axis=-1, keepdims=True)
        raised = jnp.where(visible, jnp.exp(scores - row_top), 0.0)
        return raised / jnp.sum(raised, axis=-1, keepdims=True)

    query_parts = jnp.split(queries, pieces, axis=0)
    kept, attended_parts = [], []
    for query_rows in query_parts:
        shares = shares_of(query_rows)
        attended_parts.append(product(shares.astype(bf16), values_all))
        if pieces == 1:
            kept.append(shares)

    def to_rows(parts):
        return jnp.concatenate(jnp.split(parts, H, axis=0), axis=1)

    def to_heads(rows):
        return jnp.concatenate(jnp.split(rows, H, axis=1), axis=0)

    attn_rows = to_rows(jnp.concatenate(attended_parts, axis=0).astype(bf16))
    lowrank_two = product(attn_rows, proj_into).astype(bf16)
    branch_attn = jnp.concatenate(
        [product(attn_rows, proj_one), product(attn_rows, proj_two)], axis=1
    ) + product(lowrank_two, proj_from)
    middle = residual + branch_attn
    unit_two, inverse_two = unit_rows(middle)
    normed_two = (unit_two * gain_two).astype(bf16)

    near = gather_near(normed_two)
    rows_group = jnp.concatenate(near + [shift(piece, low, 1) for piece in near], axis=0)
    back_all = lax.all_gather(
        tie(cotangent, near[1:], up_all), block_axes, axis=0, tiled=True
    )
    low_group = product(rows_group, ffn_into).astype(bf16)
    rows_joined = jnp.concatenate([rows_group, low_group], axis=1)
    gate = product_back(rows_joined, gate_all)
    up = product_back(rows_joined, up_all)
    hidden = (jax.nn.gelu(gate, approximate=True) * up).astype(bf16)
    out_terms = to_absolute(product(hidden, down_all).astype(bf16))
    mixed = lax.psum_scatter(
        tie(out_terms, back_all), block_axes, scatter_dimension=0, tiled=True
    )
    back_rows = tie(to_relative(back_all), out_terms)
    back_low = product_back(back_rows, down_from).astype(bf16)
    back_joined = jnp.concatenate([back_rows, back_low], axis=1)
    grad_hidden = product_back(back_joined, down_all)
    _, pullback = jax.vjp(lambda a, b: jax.nn.gelu(a, approximate=True) * b, gate, up)
    grad_gate, grad_up = (term.astype(bf16) for term in pullback(grad_hidden))

    row_terms = (product(grad_gate, gate_all) + product(grad_up, up_all)).astype(bf16)
    middle_column = row_terms.shape[1] // 2
    jobs = [
        ScatterNear(row_terms[:, :middle_column], (low,) + mid + upper, (low,) + highs),
        ScatterNear(row_terms[:, middle_column:], mid + upper + (low,), (low,) + highs),
    ]
    def scatter_units(terms):
        return lax.psum_scatter(terms, unit_axes, scatter_dimension=0, tiled=True)

    hidden_late, gate_late = tie((hidden, grad_gate), row_terms)
    work = (
        product_rows(hidden_late, back_joined).astype(bf16),
        product_rows(gate_late, rows_joined).astype(bf16),
    )
    arrived, (down_terms, gate_terms, mixed) = advance(*jobs, beside=(*work, mixed))
    gate_sum = scatter_units(tie(gate_terms, mixed))
    up_terms = product_rows(tie(grad_up, arrived), rows_joined).astype(bf16)
    _, up_terms = advance(*jobs, beside=up_terms)
    mixed = mixed.astype(f32)
    for _ in range(len(highs) - 1):
        advance(*jobs)
    parts = jnp.concatenate([job.result() for job in jobs], axis=1)

    lowrank_four = mixed[:, D:].astype(bf16)
    branch_ffn = mixed[:, :D] + product(lowrank_four, down_from)
    final = middle + branch_ffn
    result = final.astype(bf16)
    root_means = jnp.stack([root_mean(final), root_mean(branch_attn), root_mean(branch_ffn)])
    expand_down = product_rows(lowrank_four, cotangent)

    grad_three = parts[:, D:].astype(bf16)
    adapt_ffn = product_rows(normed_two, grad_three)
    grad_normed_two = parts[:, :D] + product_back(grad_three, ffn_into)
    gain_two_grad = jnp.sum(grad_normed_two * unit_two, axis=0)
    grad_middle = cotangent.astype(f32) + norm_back(
        grad_normed_two, unit_two, inverse_two, gain_two
    )
    grad_branch = grad_middle.astype(bf16)
    grad_two = product_back(grad_branch, proj_from).astype(bf16)
    def scatter_weights(terms, order):
        return Scatter(terms.astype(bf16), core + order, ranking)

    out_jobs = [
        scatter_weights(terms, order)
        for terms, order in zip(
            (
                product_rows(
                    attn_rows, jnp.concatenate([grad_branch[:, :half], grad_two], axis=1)
                ),
                product_rows(attn_rows, grad_branch[:, half:]),
                adapt_ffn,
            ),
            (backs[0], backs[2], backs[3]),
        )
    ]
    grad_attn = to_heads(
        (
            product_back(grad_branch[:, :half], proj_one)
            + product_back(grad_branch[:, half:], proj_two)
            + product_back(grad_two, proj_into)
        ).astype(bf16)
    )
    _, grad_attn = advance(*out_jobs, beside=grad_attn)

    scores_back, grad_keys, grad_values = [], 0.0, 0.0
    for i, query_rows in enumerate(query_parts):
        grad_rows = grad_attn[i * piece_rows : (i + 1) * piece_rows]
        shares = kept[i] if kept else shares_of(tie(query_rows, grad_rows))
        delta = jnp.sum(grad_rows.astype(f32) * attended_parts[i], axis=-1, keepdims=True)
        grad_shares = product_back(grad_rows, values_all)
        grad_scores = (shares * (grad_shares - delta)).astype(bf16)
        scores_back.append(grad_scores)
        grad_keys = grad_keys + product_rows(grad_scores, query_rows) * score_scale
        grad_values = grad_values + product_rows(shares.astype(bf16), grad_rows)
    _, (grad_keys, grad_values, gate_sum) = advance(
        *out_jobs, beside=(grad_keys.astype(bf16), grad_values.astype(bf16), gate_sum)
    )
    up_sum = scatter_units(tie(up_terms, gate_sum))
    kv_jobs = [
        Scatter(grad_keys, ("head", low) + upper + mid, row_axes),
        Scatter(grad_values, mid + (low,) + upper + ("head",), row_axes),
    ]

    def query_back(seen):
        parts, lowrank, rows = tie((scores_back, lowrank_two, grad_branch), seen)
        grad_query = jnp.concatenate([product(part, keys_all) for part in parts], axis=0)
        turned = rotate(
            grad_query.reshape(H, tokens, DH) * score_scale, cosine, -sine_part
        ).astype(bf16)
        joined = to_rows(turned.reshape(H * tokens, DH))
        return (
            joined,
            product_rows(normed_one, joined[:, :half]).astype(bf16),
            product_rows(normed_one, joined[:, half:]).astype(bf16),
            product_rows(lowrank, rows).astype(bf16),
        )

    _, (joined_q_grad, *query_terms, out_expand_terms) = advance(
        *kv_jobs, *out_jobs, beside=query_back
    )
    query_jobs = [
        scatter_weights(terms, order)
        for terms, order in zip(query_terms, (backs[0], backs[2]))
    ]
    for _ in range(steps - 2):
        advance(*kv_jobs, *out_jobs)
    advance(*kv_jobs, *query_jobs)
    keys_back, values_back = kv_jobs[0].result(), kv_jobs[1].result()
    joined_kv_grad = jnp.concatenate(
        [rotate(keys_back, cosine, -sine_part).astype(bf16), values_back.astype(bf16)], axis=1
    )
    grad_joined = jnp.concatenate([joined_q_grad, joined_kv_grad], axis=1)
    grad_one = product_back(grad_joined, qkv_from).astype(bf16)
    grad_normed_one = (
        product_back(joined_q_grad[:, :half], query_one)
        + product_back(joined_q_grad[:, half:], query_two)
        + product_back(joined_kv_grad, kv_full)
        + product_back(grad_one, qkv_into)
    )
    gain_one_grad = jnp.sum(grad_normed_one * unit_one, axis=0)
    stream_grad = grad_middle + norm_back(grad_normed_one, unit_one, inverse_one, gain_one)
    last = (
        product_rows(normed_one, jnp.concatenate([joined_kv_grad, grad_one], axis=1)).astype(bf16),
        jnp.concatenate(
            [
                product_rows(lowrank_one, grad_joined).astype(bf16),
                out_expand_terms,
                expand_down.astype(bf16),
                gain_one_grad.reshape(R, -1).astype(bf16),
                gain_two_grad.reshape(R, -1).astype(bf16),
                jnp.zeros((R, 128 - 2 * gain_columns), bf16),
            ],
            axis=1,
        ),
    )
    _, (last, up_sum) = advance(*query_jobs, beside=(last, up_sum))
    down_sum = scatter_units(tie(down_terms, up_sum))
    last_jobs = [scatter_weights(terms, order) for terms, order in zip(last, (backs[0], backs[2]))]
    for _ in range(steps - 1):
        arrived, _ = advance(*query_jobs, *last_jobs)
    gate_sum, up_sum = tie((gate_sum, up_sum), arrived)
    gateweight_grad, gateexpand_grad = pair_units(gate_sum, up_sum)
    arrived, _ = advance(*last_jobs)
    down_sum = tie(down_sum, arrived)
    downweight_grad, downadapt_grad = down_sum[:, :D].astype(f32), down_sum[:, D:].astype(f32)
    advance(*last_jobs)
    kv_grad, expand_grad = last_jobs[0].result(), last_jobs[1].result()
    gains_grad = expand_grad[:, qkv_columns + 2 * D :]
    n_gain = attn_gain.shape[0]
    return (
        result,
        stream_grad,
        gains_grad[:, :gain_columns].reshape(n_gain),
        jnp.concatenate([job.result() for job in query_jobs] + [kv_grad[:, : 2 * DH]], axis=1),
        kv_grad[:, 2 * DH : 2 * DH + R],
        expand_grad[:, :qkv_columns],
        jnp.concatenate([job.result()[:, :half] for job in out_jobs[:2]], axis=1),
        out_jobs[0].result()[:, half:],
        expand_grad[:, qkv_columns : qkv_columns + D],
        gains_grad[:, gain_columns : 2 * gain_columns].reshape(n_gain),
        gateweight_grad,
        out_jobs[2].result(),
        gateexpand_grad,
        downweight_grad,
        downadapt_grad,
        expand_grad[:, qkv_columns + D : qkv_columns + 2 * D],
        root_means,
    )


def solution(mesh):
    levels = mesh.shape["blk"].bit_length() - 1
    ranking = ("seq", "head") + tuple(f"blk{i}" for i in reversed(range(levels)))
    fine = jax.sharding.Mesh(mesh.devices.reshape((2,) * len(ranking)), ranking)
    rows = [P(ranking, *([None] * (rank - 1))) for rank in range(4)]
    in_specs = tuple(
        rows[rank] for rank in (2, 1, 2, 2, 2, 2, 2, 2, 1, 3, 2, 3, 2, 2, 2, 2)
    )
    out_specs = tuple(
        rows[rank] for rank in (2, 2, 1, 2, 2, 2, 2, 2, 2, 1, 3, 2, 3, 2, 2, 2)
    ) + (P(None, ranking),)
    return jax.shard_map(
        functools.partial(body, ranking),
        mesh=fine,
        in_specs=in_specs,
        out_specs=out_specs,
        check_vma=False,
    )
```

```python
import functools
import math

import jax
import jax.numpy as jnp
from jax import lax
from jax.experimental import pallas as pl
from jax.sharding import PartitionSpec as P

D = 2048
H = 8
DH = 256
R = 256


EPSILON = 1e-06
NEGATIVE = -1e30


def product(former, latter):
    return jnp.dot(former, latter, preferred_element_type=jnp.float32)


def product_back(former, latter):
    return lax.dot_general(
        former, latter, (((1,), (1,)), ((), ())), preferred_element_type=jnp.float32
    )


def product_rows(former, latter):
    return lax.dot_general(
        former, latter, (((0,), (0,)), ((), ())), preferred_element_type=jnp.float32
    )


def rope_tables(positions, full_width):
    half_width = full_width // 2
    rates = jnp.exp(
        jnp.arange(half_width, dtype=jnp.float32) * (-2.0 * math.log(10000.0) / full_width)
    )
    angles = positions.astype(jnp.float32)[:, None] * rates[None, :]
    return (jnp.cos(angles), jnp.sin(angles))


def rotate(values, cosine, sine_part):
    half_width = values.shape[-1] // 2
    former = values[..., :half_width]
    latter = values[..., half_width:]
    return jnp.concatenate(
        [former * cosine - latter * sine_part, latter * cosine + former * sine_part], axis=-1
    )


def unit_rows(values):
    inverse = lax.rsqrt(jnp.mean(values * values, axis=-1, keepdims=True) + EPSILON)
    return (values * inverse, inverse)


def norm_back(grad_in, scaled_rows, inverse, gain_row):
    weighted = grad_in * gain_row
    return inverse * (
        weighted - scaled_rows * jnp.mean(weighted * scaled_rows, axis=-1, keepdims=True)
    )


def root_mean(values):
    return jnp.sqrt(jnp.mean(values * values, axis=-1))


def shift(values, axes, mask):
    size = lax.axis_size(axes)
    return lax.ppermute(values, axes, [(i, i ^ mask) for i in range(size)])


def place(own, other, axis_name, position):
    first = lax.axis_index(axis_name) == 0
    return jnp.stack(
        [jnp.where(first, own, other), jnp.where(first, other, own)], axis=position
    )


class Gather:
    def __init__(self, shard, order, ranking):
        self.value, self.order, self.ranking = shard, list(order), ranking
        self.tail, self.done = shard.shape[1:], []

    def start(self):
        return shift(self.value, self.order[0], 1)

    def finish(self, other):
        name = self.order.pop(0)
        position = sum(self.ranking.index(d) < self.ranking.index(name) for d in self.done)
        self.value = place(self.value, other, name, position)
        self.done.append(name)

    def result(self):
        return self.value.reshape((-1,) + self.tail)


class Scatter:
    def __init__(self, terms, order, ranking):
        self.left = [name for name in ranking if name in order]
        self.order = list(order)
        rows = terms.shape[0] // 2 ** len(order)
        self.value = terms.reshape((2,) * len(order) + (rows,) + terms.shape[1:])

    def start(self):
        name = self.order[0]
        position, mine = self.left.index(name), lax.axis_index(name)
        sent = lax.dynamic_index_in_dim(self.value, 1 - mine, position, keepdims=False)
        return shift(sent, name, 1)

    def finish(self, other):
        name = self.order.pop(0)
        position, mine = self.left.index(name), lax.axis_index(name)
        kept = lax.dynamic_index_in_dim(self.value, mine, position, keepdims=False)
        self.value = kept.astype(jnp.float32) + other.astype(jnp.float32)
        if self.order:
            self.value = self.value.astype(jnp.bfloat16)
        self.left.remove(name)

    def result(self):
        return self.value


class ScatterNear(Scatter):
    def start(self):
        position = self.left.index(self.order[0])
        sent = lax.index_in_dim(self.value, 1, position, keepdims=False)
        return shift(sent, self.order[0], 1)

    def finish(self, other):
        name = self.order.pop(0)
        kept = lax.index_in_dim(self.value, 0, self.left.index(name), keepdims=False)
        self.value = kept.astype(jnp.float32) + other.astype(jnp.float32)
        if self.order:
            self.value = self.value.astype(jnp.bfloat16)
        self.left.remove(name)


def advance(*jobs, beside=()):
    arrived = [job.start() for job in jobs]
    if callable(beside):
        beside = beside(arrived[-1])
    arrived, beside = lax.optimization_barrier((arrived, beside))
    for job, other in zip(jobs, arrived):
        job.finish(other)
    return arrived, beside


def tie(values, *others):
    return lax.optimization_barrier((values, others))[0]


def pair_units(gate_sum, up_sum):
    units = gate_sum.shape[0]
    block = min(64, units)

    def kernel(gate_ref, up_ref, weight_ref, expand_ref):
        for k, ref in enumerate((gate_ref, up_ref)):
            terms = ref[...].astype(jnp.float32)
            weight_ref[:, k, :] = terms[:, :D]
            expand_ref[:, k, :] = terms[:, D:]

    return pl.pallas_call(
        kernel,
        grid=(units // block,),
        in_specs=[pl.BlockSpec((block, D + R), lambda i: (i, 0))] * 2,
        out_specs=[
            pl.BlockSpec((block, 2, D), lambda i: (i, 0, 0)),
            pl.BlockSpec((block, 2, R), lambda i: (i, 0, 0)),
        ],
        out_shape=[
            jax.ShapeDtypeStruct((units, 2, D), jnp.float32),
            jax.ShapeDtypeStruct((units, 2, R), jnp.float32),
        ],
        cost_estimate=pl.CostEstimate(
            flops=0, transcendentals=0, bytes_accessed=12 * units * (D + R)
        ),
    )(gate_sum, up_sum)


def body(
    ranking,
    stream,
    attn_gain,
    qkv_weight,
    qkv_adapt,
    qkv_expand,
    out_weight,
    out_adapt,
    out_expand,
    ffn_gain,
    gateup_weight,
    gateup_adapt,
    gateup_expand,
    down_weight,
    down_adapt,
    down_expand,
    cotangent,
):
    bf16 = jnp.bfloat16
    f32 = jnp.float32
    tokens = stream.shape[0]
    highs, low = ranking[2:-1], ranking[-1]
    row_axes, block_axes, unit_axes = ranking[1:], ranking[2:], ranking[:2]
    upper, mid, core = highs[:-1], highs[-1:], ("seq",)
    orders = (
        ("head",) + upper + (low,) + mid,
        ("head",) + mid + (low,) + upper,
        upper + ("head",) + mid + (low,),
        mid + ("head",) + upper + (low,),
    )
    steps = len(orders[0])
    backs = tuple(order[::-1] for order in orders)
    group = lax.axis_size(row_axes)
    planes = lax.axis_size(highs)
    plane = lax.axis_index(highs)
    side = lax.axis_index(low)
    own_pos = lax.axis_index(row_axes) * tokens + jnp.arange(tokens, dtype=jnp.int32)
    score_scale = DH ** (-0.5)
    half = H * DH // 2
    rank_rows = qkv_expand.shape[0]
    gain_columns = attn_gain.shape[0] // rank_rows

    from_row = jnp.concatenate(
        [
            qkv_expand,
            out_expand,
            down_expand,
            attn_gain.reshape(rank_rows, gain_columns),
            ffn_gain.reshape(rank_rows, gain_columns),
            jnp.zeros((rank_rows, 128 - 2 * gain_columns), bf16),
        ],
        axis=1,
    )
    jobs = [
        Gather(shard, order + core, ranking)
        for shard, order in zip(
            (
                jnp.concatenate([qkv_weight[:, 2 * half :], qkv_adapt], axis=1),
                from_row,
                qkv_weight[:, :half],
                qkv_weight[:, half : 2 * half],
            ),
            orders,
        )
    ]
    def gather_units(block):
        return lax.all_gather(block, unit_axes, axis=0, tiled=True)

    arrived, _ = advance(*jobs)
    down_all = gather_units(
        jnp.concatenate(tie((down_weight, down_adapt), arrived[0]), axis=1)
    )
    pair_weight, pair_expand = tie((gateup_weight, gateup_expand), arrived)
    pairs = [
        jnp.concatenate([pair_weight[:, k], pair_expand[:, k]], axis=1) for k in range(2)
    ]
    arrived, pairs = advance(*jobs, beside=pairs)
    for _ in range(steps - 3):
        arrived, _ = advance(*jobs)
    gate_all = gather_units(tie(pairs[0], arrived))
    arrived, down_all = advance(*jobs, beside=down_all)
    advance(*jobs[:2])
    advance(*jobs[2:])
    kv_into, from_all, query_one, query_two = (job.result() for job in jobs)
    kv_full, qkv_into = kv_into[:, : 2 * DH], kv_into[:, 2 * DH :]
    qkv_columns = 2 * half + 2 * DH
    qkv_from = from_all[:, :qkv_columns]
    proj_from = from_all[:, qkv_columns : qkv_columns + D]
    down_from = from_all[:, qkv_columns + D : qkv_columns + 2 * D]
    gains = from_all[:, qkv_columns + 2 * D :]
    gain_one = gains[:, :gain_columns].reshape(D).astype(f32)
    gain_two = gains[:, gain_columns : 2 * gain_columns].reshape(D).astype(f32)

    residual = stream.astype(f32)
    unit_one, inverse_one = unit_rows(residual)
    normed_one = (unit_one * gain_one).astype(bf16)
    lowrank_one = product(normed_one, qkv_into).astype(bf16)
    joined_kv = product(normed_one, kv_full) + product(lowrank_one, qkv_from[:, 2 * half :])
    cosine, sine_part = rope_tables(own_pos, DH)
    keys = rotate(joined_kv[:, :DH], cosine, sine_part).astype(bf16)
    values = joined_kv[:, DH:].astype(bf16)
    joined_q = jnp.concatenate(
        [product(normed_one, query_one), product(normed_one, query_two)], axis=1
    ) + product(lowrank_one, qkv_from[:, : 2 * half])
    queries = (
        rotate(jnp.stack(jnp.split(joined_q, H, axis=1)), cosine, sine_part)
        .astype(bf16)
        .reshape(H * tokens, DH)
    )

    jobs = [
        Gather(shard, order, ranking)
        for shard, order in zip(
            (
                keys,
                values,
                jnp.concatenate([out_weight[:, :half], out_adapt], axis=1),
                jnp.concatenate([out_weight[:, half:], gateup_adapt], axis=1),
            ),
            (orders[1], orders[3], orders[0] + core, orders[2] + core),
        )
    ]
    arrived, (queries, gate_all) = advance(*jobs, beside=(queries, gate_all))
    up_all = gather_units(tie(pairs[1], gate_all))
    for _ in range(steps - 2):
        arrived, _ = advance(*jobs)
    arrived, up_all = advance(*jobs, beside=up_all)
    keys_all, values_all = jobs[0].result(), jobs[1].result()
    advance(*jobs[2:])
    out_one, out_two = jobs[2].result(), jobs[3].result()
    proj_one, proj_into = out_one[:, :half], out_one[:, half:]
    proj_two, ffn_into = out_two[:, :half], out_two[:, half:]

    def gather_near(rows):
        return [rows] + [shift(rows, highs, mask) for mask in range(1, planes)]

    def to_relative(rows):
        return jnp.concatenate(
            [
                lax.dynamic_slice_in_dim(
                    rows, ((plane ^ mask) * 2 + (side ^ far)) * tokens, tokens, 0
                )
                for far in range(2)
                for mask in range(planes)
            ],
            axis=0,
        )

    def to_absolute(rows):
        return jnp.concatenate(
            [
                lax.dynamic_slice_in_dim(
                    rows, ((side ^ far) * planes + (plane ^ mask)) * tokens, tokens, 0
                )
                for mask in range(planes)
                for far in range(2)
            ],
            axis=0,
        )

    key_pos = jnp.arange(group * tokens, dtype=jnp.int32)
    pieces = max(1, group * tokens // 2048)
    piece_rows = H * tokens // pieces
    visible = jnp.tile(key_pos[None, :] <= own_pos[:, None], (H // pieces, 1))

    def shares_of(query_rows):
        scores = jnp.where(
            visible, product_back(query_rows, keys_all) * score_scale, NEGATIVE
        )
        row_top = jnp.max(scores, axis=-1, keepdims=True)
        raised = jnp.where(visible, jnp.exp(scores - row_top), 0.0)
        return raised / jnp.sum(raised, axis=-1, keepdims=True)

    query_parts = jnp.split(queries, pieces, axis=0)
    kept, attended_parts = [], []
    for query_rows in query_parts:
        shares = shares_of(query_rows)
        attended_parts.append(product(shares.astype(bf16), values_all))
        if pieces == 1:
            kept.append(shares)

    def to_rows(parts):
        return jnp.concatenate(jnp.split(parts, H, axis=0), axis=1)

    def to_heads(rows):
        return jnp.concatenate(jnp.split(rows, H, axis=1), axis=0)

    attn_rows = to_rows(jnp.concatenate(attended_parts, axis=0).astype(bf16))
    lowrank_two = product(attn_rows, proj_into).astype(bf16)
    branch_attn = jnp.concatenate(
        [product(attn_rows, proj_one), product(attn_rows, proj_two)], axis=1
    ) + product(lowrank_two, proj_from)
    middle = residual + branch_attn
    unit_two, inverse_two = unit_rows(middle)
    normed_two = (unit_two * gain_two).astype(bf16)

    near = gather_near(normed_two)
    rows_group = jnp.concatenate(near + [shift(piece, low, 1) for piece in near], axis=0)
    back_all = lax.all_gather(
        tie(cotangent, near[1:], up_all), block_axes, axis=0, tiled=True
    )
    low_group = product(rows_group, ffn_into).astype(bf16)
    rows_joined = jnp.concatenate([rows_group, low_group], axis=1)
    gate = product_back(rows_joined, gate_all)
    up = product_back(rows_joined, up_all)
    hidden = (jax.nn.gelu(gate, approximate=True) * up).astype(bf16)
    out_terms = to_absolute(product(hidden, down_all).astype(bf16))
    mixed = lax.psum_scatter(
        tie(out_terms, back_all), block_axes, scatter_dimension=0, tiled=True
    )
    back_rows = tie(to_relative(back_all), out_terms)
    back_low = product_back(back_rows, down_from).astype(bf16)
    back_joined = jnp.concatenate([back_rows, back_low], axis=1)
    grad_hidden = product_back(back_joined, down_all)
    _, pullback = jax.vjp(lambda a, b: jax.nn.gelu(a, approximate=True) * b, gate, up)
    grad_gate, grad_up = (term.astype(bf16) for term in pullback(grad_hidden))

    row_terms = (product(grad_gate, gate_all) + product(grad_up, up_all)).astype(bf16)
    middle_column = row_terms.shape[1] // 2
    jobs = [
        ScatterNear(row_terms[:, :middle_column], (low,) + mid + upper, (low,) + highs),
        ScatterNear(row_terms[:, middle_column:], mid + upper + (low,), (low,) + highs),
    ]
    def scatter_units(terms):
        return lax.psum_scatter(terms, unit_axes, scatter_dimension=0, tiled=True)

    hidden_late, gate_late = tie((hidden, grad_gate), row_terms)
    work = (
        product_rows(hidden_late, back_joined).astype(bf16),
        product_rows(gate_late, rows_joined).astype(bf16),
    )
    arrived, (down_terms, gate_terms, mixed) = advance(*jobs, beside=(*work, mixed))
    gate_sum = scatter_units(tie(gate_terms, mixed))
    up_terms = product_rows(tie(grad_up, arrived), rows_joined).astype(bf16)
    _, up_terms = advance(*jobs, beside=up_terms)
    mixed = mixed.astype(f32)
    for _ in range(len(highs) - 1):
        advance(*jobs)
    parts = jnp.concatenate([job.result() for job in jobs], axis=1)

    lowrank_four = mixed[:, D:].astype(bf16)
    branch_ffn = mixed[:, :D] + product(lowrank_four, down_from)
    final = middle + branch_ffn
    result = final.astype(bf16)
    root_means = jnp.stack([root_mean(final), root_mean(branch_attn), root_mean(branch_ffn)])
    expand_down = product_rows(lowrank_four, cotangent)

    grad_three = parts[:, D:].astype(bf16)
    adapt_ffn = product_rows(normed_two, grad_three)
    grad_normed_two = parts[:, :D] + product_back(grad_three, ffn_into)
    gain_two_grad = jnp.sum(grad_normed_two * unit_two, axis=0)
    grad_middle = cotangent.astype(f32) + norm_back(
        grad_normed_two, unit_two, inverse_two, gain_two
    )
    grad_branch = grad_middle.astype(bf16)
    grad_two = product_back(grad_branch, proj_from).astype(bf16)
    def scatter_weights(terms, order):
        return Scatter(terms.astype(bf16), core + order, ranking)

    out_jobs = [
        scatter_weights(terms, order)
        for terms, order in zip(
            (
                product_rows(
                    attn_rows, jnp.concatenate([grad_branch[:, :half], grad_two], axis=1)
                ),
                product_rows(attn_rows, grad_branch[:, half:]),
                adapt_ffn,
            ),
            (backs[0], backs[2], backs[3]),
        )
    ]
    grad_attn = to_heads(
        (
            product_back(grad_branch[:, :half], proj_one)
            + product_back(grad_branch[:, half:], proj_two)
            + product_back(grad_two, proj_into)
        ).astype(bf16)
    )
    _, grad_attn = advance(*out_jobs, beside=grad_attn)

    scores_back, grad_keys, grad_values = [], 0.0, 0.0
    for i, query_rows in enumerate(query_parts):
        grad_rows = grad_attn[i * piece_rows : (i + 1) * piece_rows]
        shares = kept[i] if kept else shares_of(tie(query_rows, grad_rows))
        delta = jnp.sum(grad_rows.astype(f32) * attended_parts[i], axis=-1, keepdims=True)
        grad_shares = product_back(grad_rows, values_all)
        grad_scores = (shares * (grad_shares - delta)).astype(bf16)
        scores_back.append(grad_scores)
        grad_keys = grad_keys + product_rows(grad_scores, query_rows) * score_scale
        grad_values = grad_values + product_rows(shares.astype(bf16), grad_rows)
    _, (grad_keys, grad_values, gate_sum) = advance(
        *out_jobs, beside=(grad_keys.astype(bf16), grad_values.astype(bf16), gate_sum)
    )
    up_sum = scatter_units(tie(up_terms, gate_sum))
    kv_jobs = [
        Scatter(grad_keys, ("head", low) + upper + mid, row_axes),
        Scatter(grad_values, mid + (low,) + upper + ("head",), row_axes),
    ]

    def query_back(seen):
        parts, lowrank, rows = tie((scores_back, lowrank_two, grad_branch), seen)
        grad_query = jnp.concatenate([product(part, keys_all) for part in parts], axis=0)
        turned = rotate(
            grad_query.reshape(H, tokens, DH) * score_scale, cosine, -sine_part
        ).astype(bf16)
        joined = to_rows(turned.reshape(H * tokens, DH))
        return (
            joined,
            product_rows(normed_one, joined[:, :half]).astype(bf16),
            product_rows(normed_one, joined[:, half:]).astype(bf16),
            product_rows(lowrank, rows).astype(bf16),
        )

    _, (joined_q_grad, *query_terms, out_expand_terms) = advance(
        *kv_jobs, *out_jobs, beside=query_back
    )
    query_jobs = [
        scatter_weights(terms, order)
        for terms, order in zip(query_terms, (backs[0], backs[2]))
    ]
    for _ in range(steps - 2):
        advance(*kv_jobs, *out_jobs)
    advance(*kv_jobs, *query_jobs)
    keys_back, values_back = kv_jobs[0].result(), kv_jobs[1].result()
    joined_kv_grad = jnp.concatenate(
        [rotate(keys_back, cosine, -sine_part).astype(bf16), values_back.astype(bf16)], axis=1
    )
    grad_joined = jnp.concatenate([joined_q_grad, joined_kv_grad], axis=1)
    grad_one = product_back(grad_joined, qkv_from).astype(bf16)
    grad_normed_one = (
        product_back(joined_q_grad[:, :half], query_one)
        + product_back(joined_q_grad[:, half:], query_two)
        + product_back(joined_kv_grad, kv_full)
        + product_back(grad_one, qkv_into)
    )
    gain_one_grad = jnp.sum(grad_normed_one * unit_one, axis=0)
    stream_grad = grad_middle + norm_back(grad_normed_one, unit_one, inverse_one, gain_one)
    last = (
        product_rows(normed_one, jnp.concatenate([joined_kv_grad, grad_one], axis=1)).astype(bf16),
        jnp.concatenate(
            [
                product_rows(lowrank_one, grad_joined).astype(bf16),
                out_expand_terms,
                expand_down.astype(bf16),
                gain_one_grad.reshape(R, -1).astype(bf16),
                gain_two_grad.reshape(R, -1).astype(bf16),
                jnp.zeros((R, 128 - 2 * gain_columns), bf16),
            ],
            axis=1,
        ),
    )
    _, (last, up_sum) = advance(*query_jobs, beside=(last, up_sum))
    down_sum = scatter_units(tie(down_terms, up_sum))
    last_jobs = [scatter_weights(terms, order) for terms, order in zip(last, (backs[0], backs[2]))]
    advance(*last_jobs)
    advance(*query_jobs)
    for _ in range(steps - 2):
        arrived, _ = advance(*query_jobs, *last_jobs)
    gate_sum, up_sum = tie((gate_sum, up_sum), arrived)
    gateweight_grad, gateexpand_grad = pair_units(gate_sum, up_sum)
    arrived, _ = advance(*last_jobs)
    down_sum = tie(down_sum, arrived)
    downweight_grad, downadapt_grad = down_sum[:, :D].astype(f32), down_sum[:, D:].astype(f32)
    advance(*last_jobs)
    kv_grad, expand_grad = last_jobs[0].result(), last_jobs[1].result()
    gains_grad = expand_grad[:, qkv_columns + 2 * D :]
    n_gain = attn_gain.shape[0]
    return (
        result,
        stream_grad,
        gains_grad[:, :gain_columns].reshape(n_gain),
        jnp.concatenate([job.result() for job in query_jobs] + [kv_grad[:, : 2 * DH]], axis=1),
        kv_grad[:, 2 * DH : 2 * DH + R],
        expand_grad[:, :qkv_columns],
        jnp.concatenate([job.result()[:, :half] for job in out_jobs[:2]], axis=1),
        out_jobs[0].result()[:, half:],
        expand_grad[:, qkv_columns : qkv_columns + D],
        gains_grad[:, gain_columns : 2 * gain_columns].reshape(n_gain),
        gateweight_grad,
        out_jobs[2].result(),
        gateexpand_grad,
        downweight_grad,
        downadapt_grad,
        expand_grad[:, qkv_columns + D : qkv_columns + 2 * D],
        root_means,
    )


def solution(mesh):
    levels = mesh.shape["blk"].bit_length() - 1
    ranking = ("seq", "head") + tuple(f"blk{i}" for i in reversed(range(levels)))
    fine = jax.sharding.Mesh(mesh.devices.reshape((2,) * len(ranking)), ranking)
    rows = [P(ranking, *([None] * (rank - 1))) for rank in range(4)]
    in_specs = tuple(
        rows[rank] for rank in (2, 1, 2, 2, 2, 2, 2, 2, 1, 3, 2, 3, 2, 2, 2, 2)
    )
    out_specs = tuple(
        rows[rank] for rank in (2, 2, 1, 2, 2, 2, 2, 2, 2, 1, 3, 2, 3, 2, 2, 2)
    ) + (P(None, ranking),)
    return jax.shard_map(
        functools.partial(body, ranking),
        mesh=fine,
        in_specs=in_specs,
        out_specs=out_specs,
        check_vma=False,
    )
```
